512 devices in a mesh: au: 16 (over y, x), vert: 32 (over z, core).
Axes of the slice: x: 4, y: 4, z: 16, core: 2. Of those that a mesh axis runs over, the one named last changes fastest.
Arguments:
- visibilities: bfloat16 [12288, 2, 2048], P(('au', 'vert')), may hold values from -6 to 6
- baseline_offsets: float32 [12288, 2, 128], P(('au', 'vert')), may hold values from -8 to 8
- channel_scale: float32 [16], replicated, may hold values from 0.8 to 1.25
- screen_depth: float32 [12288], P(('au', 'vert')), may hold values from -300 to 300
- stations: int32 [12288, 2], P(('au', 'vert')), may hold values from 0 to 511
- corners: int32 [12288, 2], P(('au', 'vert')), may hold values from 0 to 8191, as said below
- beam_terms: bfloat16 [512, 2, 1024], P(('au', 'vert')), may hold values from -5 to 5
Outputs:
- gridded: float32 [8192, 2, 8192], P('au', None, 'vert')
- dirty_image: float32 [8192, 2, 8192], P(('au', 'vert'))
The draws below stay inside these ranges and needn't reach their ends.
Inputs may be any that keep to these rules, and one draw needn't show every extreme that they name: Subgrid s belongs to block d = floor(s / 24); with d = r * 32 + c, corners[s, 0] lies in [r * 512, (r + 1) * 512) and the columns corners[s, 1] to corners[s, 1] + 31 lie inside one column tile of 256 columns. At most 2 subgrids of one block lie in one column tile; for every r one column tile holds exactly 2 subgrids of every block of that r.
All inputs are finite; a program needn't handle non-finite values.
Results may differ from the reference program's by a relative error of at most 0.039.
Values may be sent and summed in bfloat16 or wider, within the bound.
A program may use at most 64 MiB of HBM per device.

```python
import math
import jax
import jax.numpy as jnp
from jax import lax

G = 8192
SUB = 32
TIMES = 128
CHANNELS = 16
STATIONS = 512
SUB_DEV = 24
TILES_U = 16
TILES_V = 32
TILE_U = 512
TILE_V = 256
SUBGRIDS = 12288
CAP = 2


def draw_corners(key, part):
    device_total = TILES_U * TILES_V
    key_hot, key_devices = jax.random.split(jax.random.fold_in(key, 11))
    hot_columns = jax.random.randint(key_hot, (TILES_U,), 0, TILES_V)
    device_keys = jax.random.split(key_devices, device_total)

    def one_device(device_key, device):
        random_keys = jax.random.split(device_key, 5)
        row_tile = device // TILES_V
        target = hot_columns[row_tile]
        candidate_options = jnp.arange(TILES_V * CAP, dtype=jnp.int32) // CAP
        middle_point = TILES_V // 2
        extra_reward = (middle_point - jnp.abs(candidate_options - middle_point)) * 4096
        placement_score = jax.random.randint(random_keys[0], candidate_options.shape, 0, 65536) + extra_reward
        placement_score = jnp.where(candidate_options == target, -1, placement_score)
        ranked = placement_score * (TILES_V * CAP) + jnp.arange(TILES_V * CAP, dtype=jnp.int32)
        ordering = jnp.argsort(-ranked)
        chosen = candidate_options[ordering[:SUB_DEV - CAP]]
        targets = jnp.concatenate([chosen, jnp.full((CAP,), target, jnp.int32)])
        targets = targets[jax.random.permutation(random_keys[1], SUB_DEV)]
        row_offset = jax.random.randint(random_keys[2], (SUB_DEV,), 0, TILE_U)
        col_offset = jax.random.randint(random_keys[3], (SUB_DEV,), 0, TILE_V - SUB + 1)
        marks = jax.random.permutation(random_keys[4], SUB_DEV)
        row_offset = row_offset.at[marks[0]].set(0).at[marks[1]].set(TILE_U - 1)
        col_offset = col_offset.at[marks[2]].set(0).at[marks[3]].set(TILE_V - SUB)
        grid_rows = row_tile * TILE_U + row_offset
        grid_cols = targets * TILE_V + col_offset
        return jnp.stack([grid_rows, grid_cols], axis=1)
    result = jax.vmap(one_device)(device_keys, jnp.arange(device_total, dtype=jnp.int32))
    return result.reshape(device_total * SUB_DEV, 2).astype(jnp.int32)


def set_ends(values, own_key, low, largest):
    shape = values.shape
    place = [jax.random.randint(jax.random.fold_in(own_key, axis), (), 0, shape[axis]) for axis in range(len(shape))]
    values = values.at[tuple(place)].set(low)
    longest = shape.index(max(shape))
    place[longest] = (place[longest] + 1) % shape[longest]
    return values.at[tuple(place)].set(largest)


def level_of(key, dims, cuts, least, top_value):
    def one(axis_at, shards_of):
        steps = jax.random.uniform(jax.random.fold_in(jax.random.fold_in(key, 6), axis_at), (shards_of,), jnp.float32, least / len(cuts), top_value / len(cuts))
        return jnp.repeat(jnp.exp(steps), dims[axis_at] // shards_of).reshape((-1,) + (1,) * (len(dims) - axis_at - 1))

    level = one(*cuts[0])
    for cut in cuts[1:]:
        level = level * one(*cut)
    return level


def noise(stream_key, dims, width, most, cuts=(), held_as=jnp.bfloat16):
    entries = width * jax.random.normal(stream_key, dims, jnp.float32)
    if cuts:
        entries = entries * level_of(stream_key, dims, cuts, -0.22, 0.18)
    return jnp.clip(entries, -most, most).astype(held_as)


def setup_inputs(seed: int = 0) -> dict:
    key_list = jax.random.split(jax.random.key(seed), 8)
    return {
        "visibilities": noise(key_list[0], (SUBGRIDS, 2, TIMES * CHANNELS), 1.0, 6.0, ((0, 512),)),
        "baseline_offsets": jnp.clip(jax.random.uniform(key_list[1], (SUBGRIDS, 2, TIMES), jnp.float32, -8.0, 8.0) * level_of(key_list[1], (SUBGRIDS, 2, TIMES), ((0, 512),), -0.4, 0.0), -8.0, 8.0),
        "channel_scale": jnp.clip(jnp.exp(jax.random.uniform(key_list[2], (CHANNELS,), jnp.float32, math.log(0.8), math.log(1.25))), 0.8, 1.25),
        "screen_depth": jnp.clip(jax.random.uniform(key_list[3], (SUBGRIDS,), jnp.float32, -300.0, 300.0) * level_of(key_list[3], (SUBGRIDS,), ((0, 512),), -0.4, 0.0), -300.0, 300.0),
        "stations": set_ends(jax.random.randint(key_list[4], (SUBGRIDS, 2), 0, STATIONS), jax.random.fold_in(key_list[4], 1), 0, STATIONS - 1).astype(jnp.int32),
        "corners": draw_corners(jax.random.fold_in(key_list[7], 71), 0),
        "beam_terms": noise(key_list[6], (STATIONS, 2, SUB * SUB), 1.0, 5.0, ((0, 512),)),
    }


field_view = 0.1
highest = lax.Precision.HIGHEST

def complex_einsum(formula, left_operand_pair, right_pair):
    left_re, left_im = left_operand_pair
    right_re, right_im = right_pair
    real_part = jnp.einsum(formula, left_re, right_re, precision=highest) - jnp.einsum(formula, left_im, right_im, precision=highest)
    imag_part = jnp.einsum(formula, left_re, right_im, precision=highest) + jnp.einsum(formula, left_im, right_re, precision=highest)
    return (real_part, imag_part)

def complex_product(left_operand_pair, right_pair):
    return (left_operand_pair[0] * right_pair[0] - left_operand_pair[1] * right_pair[1], left_operand_pair[0] * right_pair[1] + left_operand_pair[1] * right_pair[0])

def subgrid_table():
    centred = jnp.arange(SUB, dtype=jnp.int32) - SUB // 2
    product = centred[:, None] * centred[None, :] % SUB
    angle = -2.0 * math.pi / SUB * product.astype(jnp.float32)
    return (jnp.cos(angle) / SUB, jnp.sin(angle) / SUB)

def grid_subgrids(vis_items, offset_items, depth_items, beam_first, beam_second, channel_scale):
    item_count = vis_items.shape[0]
    vis_count = vis_items.shape[2]
    pixel_pos = jnp.arange(SUB, dtype=jnp.float32) - SUB // 2
    shift_u = (offset_items[:, 0, :, None] * channel_scale[None, None, :]).reshape(item_count, vis_count)
    shift_v = (offset_items[:, 1, :, None] * channel_scale[None, None, :]).reshape(item_count, vis_count)
    angle_u = 2.0 * math.pi / SUB * pixel_pos[None, :, None] * shift_u[:, None, :]
    angle_v = 2.0 * math.pi / SUB * pixel_pos[None, :, None] * shift_v[:, None, :]
    vis_re = vis_items[:, 0, None, :].astype(jnp.float32)
    vis_im = vis_items[:, 1, None, :].astype(jnp.float32)
    cos_u = jnp.cos(angle_u)
    sin_u = jnp.sin(angle_u)
    weighted_re = (vis_re * cos_u - vis_im * sin_u).astype(jnp.bfloat16)
    weighted_im = (vis_re * sin_u + vis_im * cos_u).astype(jnp.bfloat16)
    phasor_re = jnp.cos(angle_v).astype(jnp.bfloat16)
    phasor_im = jnp.sin(angle_v).astype(jnp.bfloat16)
    sky_pair = complex_einsum('npk,nqk->npq', (weighted_re.astype(jnp.float32), weighted_im.astype(jnp.float32)), (phasor_re.astype(jnp.float32), phasor_im.astype(jnp.float32)))
    taper_line = 1.0 - ((2.0 * jnp.arange(SUB, dtype=jnp.float32) + 1.0 - SUB) / SUB) ** 2
    taper_grid = taper_line[:, None] * taper_line[None, :] / math.sqrt(vis_count)
    sky_angle = pixel_pos * field_view / SUB
    radius_sq = sky_angle[:, None] ** 2 + sky_angle[None, :] ** 2
    screen_angle = -math.pi * depth_items[:, None, None] * radius_sq[None, :, :]
    first_beam = beam_first.astype(jnp.float32).reshape(item_count, 2, SUB, SUB)
    second_beam = beam_second.astype(jnp.float32).reshape(item_count, 2, SUB, SUB)
    pair_term = complex_product((first_beam[:, 0], first_beam[:, 1]), (second_beam[:, 0], -second_beam[:, 1]))
    mixed = complex_product(sky_pair, pair_term)
    screened = complex_product(mixed, (jnp.cos(screen_angle), jnp.sin(screen_angle)))
    corrected = (screened[0] * taper_grid, screened[1] * taper_grid)
    dft_pair = subgrid_table()
    partial_pair = complex_einsum('ip,npq->niq', dft_pair, corrected)
    uv_pair = complex_einsum('niq,jq->nij', partial_pair, dft_pair)
    return jnp.stack(uv_pair, axis=1).reshape(item_count, 2 * SUB * SUB)

def reference(visibilities, baseline_offsets, channel_scale, screen_depth, stations, corners, beam_terms):
    subgrid_total = visibilities.shape[0]
    block_size = math.gcd(subgrid_total, 64)
    block_count = subgrid_total // block_size

    def grid_block(pieces):
        vis_block, offset_block, depth_block, station_block = pieces
        first_beam = jnp.take(beam_terms, station_block[:, 0], axis=0)
        second_beam = jnp.take(beam_terms, station_block[:, 1], axis=0)
        return grid_subgrids(vis_block, offset_block, depth_block, first_beam, second_beam, channel_scale).astype(jnp.bfloat16)
    gridded_blocks = lax.map(grid_block, (visibilities.reshape((block_count, block_size) + visibilities.shape[1:]), baseline_offsets.reshape((block_count, block_size) + baseline_offsets.shape[1:]), screen_depth.reshape(block_count, block_size), stations.reshape(block_count, block_size, 2)))
    uv_values = gridded_blocks.reshape(subgrid_total, 2, SUB, SUB).astype(jnp.float32)
    span_index = jnp.arange(SUB, dtype=jnp.int32)
    row_index = (corners[:, 0, None] + span_index[None, :]) % G
    col_index = corners[:, 1, None] + span_index[None, :]
    gridded = jnp.zeros((G, 2, G), jnp.float32)
    gridded = gridded.at[row_index[:, :, None], :, col_index[:, None, :]].add(jnp.transpose(uv_values, (0, 2, 3, 1)))
    uv_field = lax.complex(gridded[:, 0, :], gridded[:, 1, :])
    spectrum = jnp.fft.ifft2(uv_field) * (G * G)
    image_scale = 1.0 / (SUB * math.sqrt(SUBGRIDS))
    dirty_image = jnp.stack([jnp.real(spectrum).T, jnp.imag(spectrum).T], axis=1) * image_scale
    return (gridded, dirty_image)
```

```python
import math
import numpy as np
import jax
import jax.numpy as jnp
from jax import lax
from jax.experimental import pallas as pl
from jax.experimental.pallas import tpu as pltpu

SUB = 32
NS = 24
NK = 2048
F32 = jnp.float32
BF = jnp.bfloat16
VM = pl.BlockSpec(memory_space=pltpu.VMEM)
SM = pl.BlockSpec(memory_space=pltpu.SMEM)


def cmul(ar, ai, br, bi):
    return ar * br - ai * bi, ar * bi + ai * br


def base_phase(theta):
    t = theta * theta
    s = F32(0.0)
    for n in range(17, 1, -2):
        s = (s + F32((-1.0) ** ((n - 1) // 2) / math.factorial(n))) * t
    c = F32(0.0)
    for n in range(18, 0, -2):
        c = (c + F32((-1.0) ** (n // 2) / math.factorial(n))) * t
    return c + F32(1.0), theta * (s + F32(1.0))


def sky_kernel(vis_ref, off_ref, scale_ref, sky_ref, zu, mu, zv, wp):
    time_id = lax.broadcasted_iota(jnp.int32, (128, NK), 0)
    k_id = lax.broadcasted_iota(jnp.int32, (128, NK), 1)
    spread = (lax.shift_right_logical(k_id, 4) == time_id).astype(F32)
    scale = scale_ref[...] * F32(2.0 * math.pi / SUB)
    def put(dest, n, pair):
        for part in range(2):
            for lo in range(0, NK, 128):
                dest[n + part, lo // 128, 0:NS, :] = pair[part][:, lo:lo + 128]

    for axis in range(2):
        shift = jnp.dot(off_ref[axis], spread, precision=lax.Precision.HIGHEST, preferred_element_type=F32)
        e1 = base_phase(shift * scale)
        e2 = cmul(*e1, *e1)
        e4 = cmul(*e2, *e2)
        e8 = cmul(*e4, *e4)
        e16 = cmul(*e8, *e8)
        dest = (zu, zv)[axis]
        put(dest, 0, e1)
        put(dest, 2, e2)
        put(dest, 4, e4)
        if axis == 1:
            put(zv, 6, e8)
            put(zv, 8, e16)
        else:
            vis = vis_ref[0], vis_ref[1]
            put(mu, 0, cmul(*vis, e16[0], -e16[1]))
            put(mu, 2, cmul(*vis, e8[0], -e8[1]))
            put(mu, 4, vis)
            put(mu, 6, cmul(*vis, *e8))

    row = lax.broadcasted_iota(jnp.int32, (8, 128), 0)
    bit0, bit1, bit2 = [(lax.shift_right_logical(row, n) & 1) == 1 for n in range(3)]
    one = jnp.ones((8, 128), F32)
    zero = jnp.zeros((8, 128), F32)

    def wide(ref, n, s, lo):
        return ref[n, lo // 128, pl.ds(s, 8, stride=0), :]

    def base_tile(ref, s, lo):
        tr = jnp.where(bit0, wide(ref, 0, s, lo), one)
        ti = jnp.where(bit0, wide(ref, 1, s, lo), zero)
        tr, ti = cmul(tr, ti, jnp.where(bit1, wide(ref, 2, s, lo), one), jnp.where(bit1, wide(ref, 3, s, lo), zero))
        return cmul(tr, ti, jnp.where(bit2, wide(ref, 4, s, lo), one), jnp.where(bit2, wide(ref, 5, s, lo), zero))

    def one_subgrid(s, slot):
        for lo in range(0, NK, 128):
            br, bi = base_tile(zu, s, lo)
            blocks = [cmul(br, bi, wide(mu, 2 * n, s, lo), wide(mu, 2 * n + 1, s, lo)) for n in range(4)]
            for part in range(2):
                for half in range(2):
                    wp[slot, part * 32 + half * 16:part * 32 + half * 16 + 16, lo:lo + 128] = jnp.concatenate(
                        [blocks[2 * half][part], blocks[2 * half + 1][part]], axis=0).astype(BF)
            br, bi = base_tile(zv, s, lo)
            e8r, e8i = wide(zv, 6, s, lo), wide(zv, 7, s, lo)
            e16r, e16i = wide(zv, 8, s, lo), wide(zv, 9, s, lo)
            blocks = [cmul(br, bi, e16r, -e16i), cmul(br, bi, e8r, -e8i), (br, bi), cmul(br, bi, e8r, e8i)]
            for part in range(2):
                for half in range(2):
                    wp[slot, 64 + part * 32 + half * 16:64 + part * 32 + half * 16 + 16, lo:lo + 128] = jnp.concatenate(
                        [blocks[2 * half][part], blocks[2 * half + 1][part]], axis=0).astype(BF)

    def finish(s, slot):
        prod = lax.dot_general(wp[slot, 0:64, :], wp[slot, 64:128, :], (((1,), (1,)), ((), ())), preferred_element_type=F32)
        sky_ref[s, 0:32, :] = prod[0:32, 0:32] - prod[32:64, 32:64]
        sky_ref[s, 32:64, :] = prod[0:32, 32:64] + prod[32:64, 0:32]

    def pair(i, _):
        one_subgrid(2 * i, 0)
        one_subgrid(2 * i + 1, 1)
        finish(2 * i, 0)
        finish(2 * i + 1, 1)
        return 0

    lax.fori_loop(0, NS // 2, pair, 0)


def sky_call(vis, off, scale):
    return pl.pallas_call(
        sky_kernel,
        out_shape=jax.ShapeDtypeStruct((NS, 64, 32), F32),
        in_specs=[VM] * 3, out_specs=VM,
        scratch_shapes=[pltpu.VMEM((6, 16, 32, 128), F32), pltpu.VMEM((8, 16, 32, 128), F32), pltpu.VMEM((10, 16, 32, 128), F32),
                        pltpu.VMEM((2, 128, NK), BF)],
        name="sky",
        cost_estimate=pl.CostEstimate(flops=24 * 64 * 64 * 2048 * 2 * 20, bytes_accessed=4 << 20, transcendentals=0),
    )(vis, off, scale)


def dft_tables():
    x = np.arange(32) - 16
    phi = 2.0 * np.pi / 32 * (x[:, None] * x[None, :] % 32)
    c, s = np.cos(phi) / 32, np.sin(phi) / 32
    left = np.block([[c, s], [-s, c]])
    right = np.concatenate([c, s], axis=1)
    return left.astype(np.float32), right.astype(np.float32)


def uv_kernel(st_ref, ints_ref, depth_ref, sky_ref, beam_ref, meta_ref, left_ref, right_ref, rows_ref, slot_ref, mr_ref, g_ref, rb_ref):
    x = lax.broadcasted_iota(jnp.int32, (8, 128), 0)
    lane = lax.broadcasted_iota(jnp.int32, (8, 128), 1)
    p = 4 * x + lax.shift_right_logical(lane, 5) - 16
    q = (lane & 31) - 16
    pf, qf = p.astype(F32), q.astype(F32)
    ap, aq = pf * F32(0.1 / 32), qf * F32(0.1 / 32)
    rad = ap * ap + aq * aq
    tp = (2.0 * pf + 1.0) * F32(1.0 / 32)
    tq = (2.0 * qf + 1.0) * F32(1.0 / 32)
    taper = (1.0 - tp * tp) * (1.0 - tq * tq) * F32(1.0 / math.sqrt(NK))

    def one(s, _):
        a = beam_ref[st_ref[s, 0]].astype(F32)
        b = beam_ref[st_ref[s, 1]].astype(F32)
        pr = a[0:8] * b[0:8] + a[8:16] * b[8:16]
        pi_ = a[8:16] * b[0:8] - a[0:8] * b[8:16]
        turn = (ints_ref[0, s] * p + ints_ref[1, s] * q) & 31
        ang = turn.astype(F32) * F32(2.0 * math.pi / 32) - F32(math.pi) * depth_ref[s] * rad
        sc, ss = jnp.cos(ang) * taper, jnp.sin(ang) * taper
        mr, mi = cmul(pr, pi_, sc, ss)
        for y in range(4):
            ra = mr if y == 0 else pltpu.roll(mr, 128 - 32 * y, 1)
            rb = mi if y == 0 else pltpu.roll(mi, 128 - 32 * y, 1)
            mr_ref[pl.ds(y, 8, stride=4), :] = ra
            mr_ref[pl.ds(32 + y, 8, stride=4), :] = rb
        kr, ki = mr_ref[0:32, 0:32], mr_ref[32:64, 0:32]
        sr, si = sky_ref[s, 0:32, :], sky_ref[s, 32:64, :]
        cr, ci = cmul(sr, si, kr, ki)
        cor = jnp.concatenate([cr, ci], axis=0).astype(BF)
        g = jnp.dot(left_ref[...], cor, preferred_element_type=F32)
        g_ref[pl.ds(pl.multiple_of(s * 64, 64), 64), :] = g.astype(BF)
        return 0

    lax.fori_loop(0, NS, one, 0, unroll=2)

    slot_ref[...] = jnp.zeros_like(slot_ref)
    wide_lane = lax.broadcasted_iota(jnp.int32, (32, 128), 1)
    note_lane = lax.broadcasted_iota(jnp.int32, (16, 128), 1)

    def two(y, _):
        outs = []
        for half in range(2):
            s = y + 12 * half
            yv = jnp.dot(g_ref[pl.ds(pl.multiple_of(s * 64, 64), 64), :], right_ref[...], preferred_element_type=F32)
            re = yv[0:32, 0:32] + yv[32:64, 32:64]
            im = yv[32:64, 0:32] - yv[0:32, 32:64]
            both = jnp.concatenate([re, im], axis=1)
            outs.append(both)
            dest, rank = ints_ref[2, s], ints_ref[3, s]
            mine = lax.shift_right_logical(wide_lane, 6) == rank
            held = slot_ref[dest, 0:32, :].astype(F32)
            slot_ref[dest, 0:32, :] = jnp.where(mine, jnp.concatenate([both, both], axis=1), held).astype(BF)
            notes = slot_ref[dest, 32:48, :].astype(F32)
            for n in range(3):
                notes = jnp.where(note_lane == rank * 64 + n, ints_ref[4 + n, s].astype(F32), notes)
            slot_ref[dest, 32:48, :] = notes.astype(BF)
        rb_ref[pl.ds(y, 32, stride=16), :] = jnp.concatenate(outs, axis=1)
        return 0

    lax.fori_loop(0, 12, two, 0)
    for n in range(4):
        rb_ref[pl.ds(12 + n, 32, stride=16), :] = jnp.broadcast_to(meta_ref[n:n + 1, :], (32, 128))
    rows_ref[...] = rb_ref[...].astype(BF)


def uv_call(stations, ints, depth, sky, beam, meta):
    left, right = dft_tables()
    return pl.pallas_call(
        uv_kernel,
        out_shape=(jax.ShapeDtypeStruct((512, 128), BF), jax.ShapeDtypeStruct((32, 48, 128), BF)),
        in_specs=[SM] * 3 + [VM] * 5, out_specs=(VM, VM),
        scratch_shapes=[pltpu.VMEM((64, 128), F32), pltpu.VMEM((NS * 64, 32), BF), pltpu.VMEM((512, 128), F32)],
        name="uv",
    )(stations, ints, depth, sky, beam, meta, jnp.asarray(left, BF), jnp.asarray(right, BF))


def phase_table(rows, cols, period):
    phi = 2.0 * np.pi / period * (np.arange(rows)[:, None] * np.arange(cols)[None, :] % period)
    return np.cos(phi), np.sin(phi)


NG = 17
MSG = 48


def row_kernel(me_ref, recv_ref, stage1_ref, twist_ref, stage2_ref, out_ref, scr, lhs, oht, yv, buf):
    scr[...] = recv_ref[...].astype(F32)
    lane = lax.broadcasted_iota(jnp.int32, (32, 768), 1)
    src = lax.broadcasted_iota(jnp.int32, (32, 768), 0)
    pick_src = ((lane & 31) == src).astype(BF)
    pick_item = lax.shift_right_logical(lane, 5) == src

    def meta(n):
        table = jnp.transpose(scr[pl.ds(12 + n, 32, stride=16), :])[0:32]
        spread = jnp.dot(table.astype(BF), pick_src, preferred_element_type=F32)
        return jnp.sum(jnp.where(pick_item, spread, 0.0), axis=0, keepdims=True)

    g_hi, g_lo, h, e = [meta(n) for n in range(4)]
    me = me_ref[0].astype(F32)
    g = g_hi + jnp.where(g_lo > me, 1.0, 0.0)
    h_id = lax.broadcasted_iota(jnp.int32, (256, 768), 0).astype(F32)
    oht[:, 0:768] = (h_id == h).astype(BF)
    oht[:, 768:1536] = (h_id == h + 1.0).astype(BF)
    col = (lax.broadcasted_iota(jnp.int32, (64, 384), 0) & 31).astype(F32)
    for half in range(2):
        parts = []
        for blk in range(3):
            rows = jnp.concatenate([scr[pl.ds(4 * blk + n, 32, stride=16), :] for n in range(4)], axis=0)
            parts.append(jnp.transpose(rows)[half * 64:half * 64 + 64])
        v = jnp.concatenate(parts, axis=1)
        at = half * 384
        first = col >= e[:, at:at + 384]
        hi = jnp.where(first, v, 0.0)
        lo = jnp.where(first, 0.0, v)
        for n in range(NG):
            here = g[:, at:at + 384] == float(n)
            lhs[n * 64:n * 64 + 64, at:at + 384] = jnp.where(here, hi, 0.0).astype(BF)
            lhs[n * 64:n * 64 + 64, 768 + at:768 + at + 384] = jnp.where(here, lo, 0.0).astype(BF)
    x = lax.dot_general(lhs[...], oht[...], (((1,), (1,)), ((), ())), preferred_element_type=F32).astype(BF)
    yv[...] = jnp.dot(x, stage1_ref[...], preferred_element_type=F32)
    for n in range(NG):
        y = yv[n * 64:n * 64 + 64, :]
        re = y[0:32, 0:256] - y[32:64, 256:512]
        im = y[0:32, 256:512] + y[32:64, 0:256]
        re, im = cmul(re, im, twist_ref[0], twist_ref[1])
        z = jnp.dot(stage2_ref[...], jnp.concatenate([re, im], axis=0).astype(BF), preferred_element_type=F32)
        for low in range(2):
            for comp in range(2):
                row = comp * 16 + n if n < 16 else 32 + comp
                for k in range(2):
                    at = (low * 2 + comp) * 16
                    buf[low * 2 + k, pl.ds(row, 16, stride=MSG), :] = z[at:at + 16, k * 128:k * 128 + 128]
    for k in range(4):
        out_ref[:, k * 128:k * 128 + 128] = buf[k].astype(BF)


def row_tables():
    c, s = phase_table(256, 256, 256)
    stage1 = np.concatenate([c, s], axis=1)
    twist = np.stack(phase_table(32, 256, 8192))
    c, s = phase_table(32, 32, 32)
    full = np.stack([np.concatenate([c, -s], axis=1), np.concatenate([s, c], axis=1)])
    stage2 = full.reshape(2, 16, 2, 64).transpose(2, 0, 1, 3).reshape(64, 64)
    return stage1, twist, stage2


def row_call(me, recv):
    stage1, twist, stage2 = row_tables()
    return pl.pallas_call(
        row_kernel,
        out_shape=jax.ShapeDtypeStruct((16 * MSG, 512), BF),
        in_specs=[SM] + [VM] * 4, out_specs=VM,
        scratch_shapes=[pltpu.VMEM((512, 128), F32), pltpu.VMEM((NG * 64, 1536), BF), pltpu.VMEM((256, 1536), BF),
                        pltpu.VMEM((NG * 64, 512), F32), pltpu.VMEM((4, 16 * MSG, 128), F32)],
        name="rows",
    )(me, recv, jnp.asarray(stage1, BF), jnp.asarray(twist, F32), jnp.asarray(stage2, BF))


def high_kernel(me_ref, recv_ref, table_ref, out_ref, xh):
    first = lax.broadcasted_iota(jnp.int32, (16, 512), 0) == 0
    for r in range(16):
        for comp in range(2):
            block = recv_ref[r * MSG + comp * 16:r * MSG + comp * 16 + 16, :].astype(F32)
            before = ((r + 15) % 16) * MSG + 32
            spill = recv_ref[before:before + 16, :].astype(F32)[comp:comp + 1]
            xh[comp * 256 + r * 16:comp * 256 + r * 16 + 16, :] = jnp.where(first, block + spill, block).astype(BF)
    y = lax.dot_general(xh[...], table_ref[...], (((0,), (0,)), ((), ())), preferred_element_type=F32)
    ql = lax.broadcasted_iota(jnp.int32, (8, 256), 1)
    ang = (ql * me_ref[0]).astype(F32) * F32(2.0 * math.pi / 8192)
    re, im = cmul(y[:, 0:256], y[:, 256:512], jnp.cos(ang)[0:1], jnp.sin(ang)[0:1])
    out_ref[:, 0:256] = re.astype(BF)
    out_ref[:, 256:512] = im.astype(BF)


def high_call(me, recv):
    c, s = phase_table(256, 256, 256)
    table = np.block([[c, s], [-s, c]])
    return pl.pallas_call(
        high_kernel,
        out_shape=jax.ShapeDtypeStruct((512, 512), BF),
        in_specs=[SM] + [VM] * 2, out_specs=VM,
        scratch_shapes=[pltpu.VMEM((512, 512), BF)],
        name="high",
    )(me, recv, jnp.asarray(table, BF))


def low_kernel(recv_ref, table_ref, out_ref, scr):
    for k in range(4):
        scr[k] = recv_ref[:, k * 128:k * 128 + 128].astype(F32)
    for m in range(16):
        parts = [jnp.concatenate([scr[2 * comp + k, pl.ds(m, 32, stride=16), :] for k in range(2)], axis=1) for comp in range(2)]
        x = jnp.concatenate(parts, axis=0).astype(BF)
        out_ref[m] = jnp.dot(table_ref[...], x, preferred_element_type=F32) * F32(1.0 / (SUB * math.sqrt(12288)))


def low_call(recv):
    c, s = phase_table(32, 32, 32)
    table = np.block([[c, -s], [s, c]])
    return pl.pallas_call(
        low_kernel,
        out_shape=jax.ShapeDtypeStruct((16, 64, 256), F32),
        in_specs=[VM] * 2, out_specs=VM,
        scratch_shapes=[pltpu.VMEM((4, 512, 128), F32)],
        name="low",
    )(recv, jnp.asarray(table, BF))


def tile_kernel(notes_ref, recv_ref, rep_ref, acc_ref):
    acc_ref[...] = jnp.zeros_like(acc_ref)
    row = lax.broadcasted_iota(jnp.int32, (32, 256), 0)
    column = lax.broadcasted_iota(jnp.int32, (32, 256), 1)

    def one(n, _):
        wide = jnp.dot(recv_ref[n, 0:32, :], rep_ref[...], preferred_element_type=F32)
        for rank in range(2):
            hi, lo, start = [notes_ref[n, rank * 3 + k] for k in range(3)]
            seen = (column >= start) & (column < start + 32)
            upper = seen & (row >= lo)
            lower = seen & (row < lo)
            for comp in range(2):
                x = wide[:, (rank * 2 + comp) * 256:(rank * 2 + comp) * 256 + 256]
                acc_ref[hi, comp] += jnp.where(upper, x, 0.0)
                acc_ref[hi + 1, comp] += jnp.where(lower, x, 0.0)
        return 0

    lax.fori_loop(0, 32, one, 0)


def tile_call(notes, recv):
    rep = np.zeros((128, 1024), np.float32)
    for part in range(4):
        for v in range(256):
            rep[part * 32 + v % 32, part * 256 + v] = 1.0
    return pl.pallas_call(
        tile_kernel,
        out_shape=jax.ShapeDtypeStruct((NG, 2, 32, 256), F32),
        in_specs=[SM] + [VM] * 2, out_specs=VM,
        name="tile",
    )(notes, recv, jnp.asarray(rep, BF))


def gather_beams(beam_terms):
    table = lax.all_gather(beam_terms.reshape(1, 16, 128), "vert", axis=0, tiled=True)
    return lax.all_gather(table, "au", axis=0, tiled=True)


def exchange(value, axis, parts):
    rows, cols = value.shape
    return lax.all_to_all(value.reshape(parts, rows // parts, cols), axis, split_axis=0, concat_axis=0, tiled=True).reshape(rows, cols)


def on_device(visibilities, baseline_offsets, channel_scale, screen_depth, stations, corners, beam_terms):
    au, vert = lax.axis_index("au"), lax.axis_index("vert")
    me = vert.astype(jnp.int32).reshape(1)
    beams = gather_beams(beam_terms)
    row, col = corners[:, 0], corners[:, 1]
    dest = col // 256
    order = jnp.arange(NS, dtype=jnp.int32)
    rank = jnp.sum(((dest[None, :] == dest[:, None]) & (order[None, :] < order[:, None])).astype(jnp.int32), axis=1)
    hi, lo = (row - au * 512) // 32, row % 32
    ints = jnp.stack([row, col, dest, rank, hi, lo, col % 256])
    meta = jnp.pad(jnp.stack([hi, lo, col // 32, col % 32]).astype(F32), ((0, 0), (0, 128 - NS)))
    sky = sky_call(
        visibilities.transpose(1, 0, 2).astype(F32),
        baseline_offsets.transpose(1, 0, 2),
        jnp.broadcast_to(channel_scale[None, :], (128, 16)).reshape(1, NK),
    )
    rows, slots = uv_call(stations, ints, screen_depth, sky, beams, meta)
    rows = exchange(rows, "vert", 32)
    slots = lax.all_to_all(slots, "vert", split_axis=0, concat_axis=0, tiled=True)
    high_in = exchange(row_call(me, rows), "au", 16)
    low_in = exchange(high_call(me, high_in), "vert", 32)
    dirty = low_call(low_in).reshape(16, 2, 8192)
    notes = slots[:, 32, :]
    notes = jnp.concatenate([notes[:, 0:3], notes[:, 64:67]], axis=1).astype(jnp.int32)
    tile = tile_call(notes, slots)
    spill = lax.ppermute(tile[16].astype(BF), "au", [(n, (n + 1) % 16) for n in range(16)])
    first = tile[0] + spill.astype(F32)
    gridded = jnp.concatenate([first[None], tile[1:16]], axis=0).transpose(0, 2, 1, 3).reshape(512, 2, 256)
    return gridded, dirty


def solution(mesh):
    from jax.sharding import PartitionSpec as P

    both = ("au", "vert")
    return jax.shard_map(
        on_device,
        mesh=mesh,
        in_specs=(P(both, None, None), P(both, None, None), P(), P(both), P(both, None), P(both, None), P(both, None, None)),
        out_specs=(P("au", None, "vert"), P(both, None, None)),
        check_vma=False,
    )
```

```python
import math
import numpy as np
import jax
import jax.numpy as jnp
from jax import lax
from jax.experimental import pallas as pl
from jax.experimental.pallas import tpu as pltpu

SUB = 32
NS = 24
NK = 2048
F32 = jnp.float32
BF = jnp.bfloat16
VM = pl.BlockSpec(memory_space=pltpu.VMEM)
SM = pl.BlockSpec(memory_space=pltpu.SMEM)


def cmul(ar, ai, br, bi):
    return ar * br - ai * bi, ar * bi + ai * br


def base_phase(theta):
    t = theta * theta
    s = F32(0.0)
    for n in range(17, 1, -2):
        s = (s + F32((-1.0) ** ((n - 1) // 2) / math.factorial(n))) * t
    c = F32(0.0)
    for n in range(18, 0, -2):
        c = (c + F32((-1.0) ** (n // 2) / math.factorial(n))) * t
    return c + F32(1.0), theta * (s + F32(1.0))


def dft_tables():
    x = np.arange(32) - 16
    phi = 2.0 * np.pi / 32 * (x[:, None] * x[None, :] % 32)
    c, s = np.cos(phi) / 32, np.sin(phi) / 32
    left = np.block([[c, s], [-s, c]])
    right = np.concatenate([c, s], axis=1)
    return left.astype(np.float32), right.astype(np.float32)


def phase_table(rows, cols, period):
    phi = 2.0 * np.pi / period * (np.arange(rows)[:, None] * np.arange(cols)[None, :] % period)
    return np.cos(phi), np.sin(phi)


NG = 17


def row_tables():
    c, s = phase_table(256, 256, 256)
    stage1 = np.concatenate([c, s], axis=1)
    twist = np.stack(phase_table(32, 256, 8192))
    c, s = phase_table(32, 32, 32)
    full = np.stack([np.concatenate([c, -s], axis=1), np.concatenate([s, c], axis=1)])
    stage2 = full.reshape(2, 16, 2, 64).transpose(2, 0, 1, 3).reshape(64, 64)
    return stage1, twist, stage2


def high_table():
    c, s = phase_table(256, 256, 256)
    return np.block([[c, s], [-s, c]])


def low_table():
    c, s = phase_table(32, 32, 32)
    return np.block([[c, -s], [s, c]])


def step_setup(vis_ref, off_ref, scale_ref, zu, mu, zv):
    time_id = lax.broadcasted_iota(jnp.int32, (128, NK), 0)
    k_id = lax.broadcasted_iota(jnp.int32, (128, NK), 1)
    spread = (lax.shift_right_logical(k_id, 4) == time_id).astype(F32)
    scale = scale_ref[...] * F32(2.0 * math.pi / SUB)

    def put(dest, n, pair):
        for part in range(2):
            for lo in range(0, NK, 128):
                dest[n + part, lo // 128, 0:NS, :] = pair[part][:, lo:lo + 128]

    for axis in range(2):
        shift = jnp.dot(off_ref[axis], spread, precision=lax.Precision.HIGHEST, preferred_element_type=F32)
        e1 = base_phase(shift * scale)
        e2 = cmul(*e1, *e1)
        e4 = cmul(*e2, *e2)
        e8 = cmul(*e4, *e4)
        e16 = cmul(*e8, *e8)
        dest = (zu, zv)[axis]
        put(dest, 0, e1)
        put(dest, 2, e2)
        put(dest, 4, e4)
        if axis == 1:
            put(zv, 6, e8)
            put(zv, 8, e16)
        else:
            vis = vis_ref[0], vis_ref[1]
            put(mu, 0, cmul(*vis, e16[0], -e16[1]))
            put(mu, 2, cmul(*vis, e8[0], -e8[1]))
            put(mu, 4, vis)
            put(mu, 6, cmul(*vis, *e8))


def step_sky(first, last, zu, mu, zv, wp, sky):
    row = lax.broadcasted_iota(jnp.int32, (8, 128), 0)
    bit0, bit1, bit2 = [(lax.shift_right_logical(row, n) & 1) == 1 for n in range(3)]
    one = jnp.ones((8, 128), F32)
    zero = jnp.zeros((8, 128), F32)

    def wide(ref, n, s, chunk):
        return ref[n, chunk, pl.ds(s, 8, stride=0), :]

    def base_tile(ref, s, ch):
        tr = jnp.where(bit0, wide(ref, 0, s, ch), one)
        ti = jnp.where(bit0, wide(ref, 1, s, ch), zero)
        tr, ti = cmul(tr, ti, jnp.where(bit1, wide(ref, 2, s, ch), one), jnp.where(bit1, wide(ref, 3, s, ch), zero))
        return cmul(tr, ti, jnp.where(bit2, wide(ref, 4, s, ch), one), jnp.where(bit2, wide(ref, 5, s, ch), zero))

    def one_subgrid(s, slot):
        for ch in range(NK // 128):
            lo = ch * 128
            br, bi = base_tile(zu, s, ch)
            left = [cmul(br, bi, wide(mu, 2 * n, s, ch), wide(mu, 2 * n + 1, s, ch)) for n in range(4)]
            br, bi = base_tile(zv, s, ch)
            e8r, e8i = wide(zv, 6, s, ch), wide(zv, 7, s, ch)
            e16r, e16i = wide(zv, 8, s, ch), wide(zv, 9, s, ch)
            right = [cmul(br, bi, e16r, -e16i), cmul(br, bi, e8r, -e8i), (br, bi), cmul(br, bi, e8r, e8i)]
            for side, blocks in enumerate((left, right)):
                for part in range(2):
                    for half in range(2):
                        at = side * 64 + part * 32 + half * 16
                        wp[slot, at:at + 16, lo:lo + 128] = jnp.concatenate(
                            [blocks[2 * half][part], blocks[2 * half + 1][part]], axis=0).astype(BF)

    def finish(s, slot):
        prod = lax.dot_general(wp[slot, 0:64, :], wp[slot, 64:128, :], (((1,), (1,)), ((), ())), preferred_element_type=F32)
        sky[s, 0:32, :] = prod[0:32, 0:32] - prod[32:64, 32:64]
        sky[s, 32:64, :] = prod[0:32, 32:64] + prod[32:64, 0:32]

    def pair(i, _):
        one_subgrid(2 * i, 0)
        one_subgrid(2 * i + 1, 1)
        finish(2 * i, 0)
        finish(2 * i + 1, 1)
        return 0

    lax.fori_loop(first, last, pair, 0)


def pixel_ids():
    x = lax.broadcasted_iota(jnp.int32, (8, 128), 0)
    lane = lax.broadcasted_iota(jnp.int32, (8, 128), 1)
    return 4 * x + lax.shift_right_logical(lane, 5) - 16, (lane & 31) - 16


def unfold(re, im, box):
    for y in range(4):
        ra = re if y == 0 else pltpu.roll(re, 128 - 32 * y, 1)
        rb = im if y == 0 else pltpu.roll(im, 128 - 32 * y, 1)
        box[pl.ds(y, 8, stride=4), :] = ra
        box[pl.ds(32 + y, 8, stride=4), :] = rb
    return box[0:32, 0:32], box[32:64, 0:32]


def step_screen(ints_ref, depth_ref, sky, box):
    p, q = pixel_ids()
    pf, qf = p.astype(F32), q.astype(F32)
    ap, aq = pf * F32(0.1 / 32), qf * F32(0.1 / 32)
    rad = ap * ap + aq * aq
    tp = (2.0 * pf + 1.0) * F32(1.0 / 32)
    tq = (2.0 * qf + 1.0) * F32(1.0 / 32)
    taper = (1.0 - tp * tp) * (1.0 - tq * tq) * F32(1.0 / math.sqrt(NK))

    def one(s, _):
        turn = (ints_ref[0, s] * p + ints_ref[1, s] * q) & 31
        ang = turn.astype(F32) * F32(2.0 * math.pi / 32) - F32(math.pi) * depth_ref[s] * rad
        kr, ki = unfold(jnp.cos(ang) * taper, jnp.sin(ang) * taper, box)
        cr, ci = cmul(sky[s, 0:32, :], sky[s, 32:64, :], kr, ki)
        sky[s, 0:32, :] = cr
        sky[s, 32:64, :] = ci
        return 0

    lax.fori_loop(0, NS, one, 0)


def step_uv(ints_ref, sky, table, meta_ref, left_ref, right_ref, box, g_ref, rb):
    def one(s, _):
        a = table[ints_ref[2, s]].astype(F32)
        b = table[ints_ref[3, s]].astype(F32)
        pr = a[0:8] * b[0:8] + a[8:16] * b[8:16]
        pi_ = a[8:16] * b[0:8] - a[0:8] * b[8:16]
        kr, ki = unfold(pr, pi_, box)
        cr, ci = cmul(sky[s, 0:32, :], sky[s, 32:64, :], kr, ki)
        cor = jnp.concatenate([cr, ci], axis=0).astype(BF)
        g = jnp.dot(left_ref[...], cor, preferred_element_type=F32)
        g_ref[pl.ds(pl.multiple_of(s * 64, 64), 64), :] = g.astype(BF)
        return 0

    lax.fori_loop(0, NS, one, 0)

    def two(y, _):
        outs = []
        for half in range(2):
            s = y + 12 * half
            yv = jnp.dot(g_ref[pl.ds(pl.multiple_of(s * 64, 64), 64), :], right_ref[...], preferred_element_type=F32)
            outs.append(yv[0:32, 0:32] + yv[32:64, 32:64])
            outs.append(yv[32:64, 0:32] - yv[0:32, 32:64])
        rb[pl.ds(y, 32, stride=16), :] = jnp.concatenate(outs, axis=1)
        return 0

    lax.fori_loop(0, 12, two, 0)
    for n in range(4):
        rb[pl.ds(12 + n, 32, stride=16), :] = jnp.broadcast_to(meta_ref[n:n + 1, :], (32, 128))


def step_slots(rb, place_ref, scr, slot_send):
    low = lax.broadcasted_iota(jnp.int32, (32, 128), 1) < 64

    def one(c, _):
        x = rb[pl.ds(pl.multiple_of(c * 16, 16), 16), :]
        both = jnp.concatenate([x, pltpu.roll(x, 64, 1)], axis=0).astype(BF)
        z = jnp.dot(place_ref[...], both, preferred_element_type=F32)
        scr[pl.ds(c, 32, stride=32), :] = jnp.where(low, z[0:32], z[32:64])
        return 0

    lax.fori_loop(0, 32, one, 0)
    slot_send[...] = scr[...].reshape(32, 32, 128).astype(BF)


def step_rows(me, rows_recv, stage1_ref, twist_ref, stage2_ref, scr, lhs, oht, yv, buf, sbuf, high_send, spill_send):
    scr[...] = rows_recv[...].reshape(512, 128).astype(F32)
    lane = lax.broadcasted_iota(jnp.int32, (32, 768), 1)
    src = lax.broadcasted_iota(jnp.int32, (32, 768), 0)
    pick_src = ((lane & 31) == src).astype(BF)
    pick_item = lax.shift_right_logical(lane, 5) == src

    def meta(n):
        table = jnp.transpose(scr[pl.ds(12 + n, 32, stride=16), :])[0:32]
        spread = jnp.dot(table.astype(BF), pick_src, preferred_element_type=F32)
        return jnp.sum(jnp.where(pick_item, spread, 0.0), axis=0, keepdims=True)

    g_hi, g_lo, h, e = [meta(n) for n in range(4)]
    g = g_hi + jnp.where(g_lo > me.astype(F32), 1.0, 0.0)
    h_id = lax.broadcasted_iota(jnp.int32, (256, 768), 0).astype(F32)
    oht[:, 0:768] = (h_id == h).astype(BF)
    oht[:, 768:1536] = (h_id == h + 1.0).astype(BF)
    col = (lax.broadcasted_iota(jnp.int32, (64, 384), 0) & 31).astype(F32)
    for half in range(2):
        parts = []
        for blk in range(3):
            rows = jnp.concatenate([scr[pl.ds(4 * blk + n, 32, stride=16), :] for n in range(4)], axis=0)
            parts.append(jnp.transpose(rows)[half * 64:half * 64 + 64])
        v = jnp.concatenate(parts, axis=1)
        at = half * 384
        first = col >= e[:, at:at + 384]
        hi = jnp.where(first, v, 0.0)
        lo = jnp.where(first, 0.0, v)
        for n in range(NG):
            here = g[:, at:at + 384] == float(n)
            lhs[n * 64:n * 64 + 64, at:at + 384] = jnp.where(here, hi, 0.0).astype(BF)
            lhs[n * 64:n * 64 + 64, 768 + at:768 + at + 384] = jnp.where(here, lo, 0.0).astype(BF)
    x = lax.dot_general(lhs[...], oht[...], (((1,), (1,)), ((), ())), preferred_element_type=F32).astype(BF)
    yv[...] = jnp.dot(x, stage1_ref[...], preferred_element_type=F32)
    for n in range(NG):
        y = yv[n * 64:n * 64 + 64, :]
        re = y[0:32, 0:256] - y[32:64, 256:512]
        im = y[0:32, 256:512] + y[32:64, 0:256]
        re, im = cmul(re, im, twist_ref[0], twist_ref[1])
        z = jnp.dot(stage2_ref[...], jnp.concatenate([re, im], axis=0).astype(BF), preferred_element_type=F32)
        for low in range(2):
            for comp in range(2):
                for k in range(2):
                    at = (low * 2 + comp) * 16
                    piece = z[at:at + 16, k * 128:k * 128 + 128]
                    if n < 16:
                        buf[low * 2 + k, pl.ds(comp * 16 + n, 16, stride=32), :] = piece
                    else:
                        sbuf[pl.ds(comp * 4 + low * 2 + k, 16, stride=16), :] = piece
    for k in range(4):
        high_send[:, :, k * 128:k * 128 + 128] = buf[k].reshape(16, 32, 128).astype(BF)
    spill_send[...] = sbuf[...].reshape(16, 16, 128).astype(BF)


def step_high(me, high_recv, spill_recv, table_ref, xh, low_send):
    first = lax.broadcasted_iota(jnp.int32, (16, 512), 0) == 0
    for r in range(16):
        spill = spill_recv[(r + 15) % 16].astype(F32)
        for comp in range(2):
            block = high_recv[r, comp * 16:comp * 16 + 16, :].astype(F32)
            line = jnp.concatenate([spill[comp * 4 + k:comp * 4 + k + 1] for k in range(4)], axis=1)
            xh[comp * 256 + r * 16:comp * 256 + r * 16 + 16, :] = jnp.where(first, block + line, block).astype(BF)
    y = lax.dot_general(xh[...], table_ref[...], (((0,), (0,)), ((), ())), preferred_element_type=F32)
    ql = lax.broadcasted_iota(jnp.int32, (8, 256), 1)
    ang = (ql * me).astype(F32) * F32(2.0 * math.pi / 8192)
    re, im = cmul(y[:, 0:256], y[:, 256:512], jnp.cos(ang)[0:1], jnp.sin(ang)[0:1])
    low_send[:, :, 0:256] = re.reshape(32, 16, 256).astype(BF)
    low_send[:, :, 256:512] = im.reshape(32, 16, 256).astype(BF)


def step_low(low_recv, table_ref, scr, out_ref):
    for k in range(4):
        scr[k] = low_recv[:, :, k * 128:k * 128 + 128].reshape(512, 128).astype(F32)
    for m in range(16):
        parts = [jnp.concatenate([scr[2 * comp + k, pl.ds(m, 32, stride=16), :] for k in range(2)], axis=1) for comp in range(2)]
        x = jnp.concatenate(parts, axis=0).astype(BF)
        out_ref[m] = jnp.dot(table_ref[...], x, preferred_element_type=F32) * F32(1.0 / (SUB * math.sqrt(12288)))


def step_tile(me, scr, slot_recv, vals, spare, tile_ref, tail_send):
    vals[...] = slot_recv[...].reshape(1024, 128).astype(F32)
    hi, lo, h, e = [scr[pl.ds(12 + n, 32, stride=16), :] for n in range(4)]
    lane = lax.broadcasted_iota(jnp.int32, (32, 128), 1)
    base = me.astype(F32) * 8.0
    mine = (h >= base) & (h < base + 8.0) & (lane < NS)
    upto = (lax.broadcasted_iota(jnp.int32, (128, 128), 0) < lax.broadcasted_iota(jnp.int32, (128, 128), 1)).astype(BF)
    order = jnp.dot(mine.astype(BF), upto, preferred_element_type=F32)
    start = (h - base) * 32.0 + e
    column = lax.broadcasted_iota(jnp.int32, (32, 256), 1).astype(F32)
    seen, his, los = [], [], []
    for rank in range(2):
        pick = mine & (order == float(rank))
        hit = jnp.sum(jnp.where(pick, 1.0, 0.0), axis=1, keepdims=True)
        low_edge = jnp.sum(jnp.where(pick, start, 0.0), axis=1, keepdims=True)
        seen.append((column >= low_edge) & (column < low_edge + 32.0 * hit))
        for box, values in ((his, hi), (los, lo)):
            one = jnp.sum(jnp.where(pick, values, 0.0), axis=1, keepdims=True)
            box.append(jnp.transpose(jnp.broadcast_to(one, (32, 128)))[0:1, :])
    hi_line = jnp.concatenate(his, axis=1)
    lo_line = jnp.concatenate(los, axis=1)
    g_id = lax.broadcasted_iota(jnp.int32, (32, 64), 0).astype(F32)
    quarter = lax.shift_right_logical(lane, 5)

    def one(c, _):
        x = vals[pl.ds(c, 32, stride=32), :]
        lines = []
        for rank in range(2):
            for comp in range(2):
                y = jnp.where(quarter == rank * 2 + comp, x, 0.0)
                y = y + pltpu.roll(y, 32, 1)
                y = y + pltpu.roll(y, 64, 1)
                lines.append(jnp.where(seen[rank], jnp.concatenate([y, y], axis=1), 0.0))
        rhs = jnp.concatenate([jnp.concatenate(lines[0:2], axis=1), jnp.concatenate(lines[2:4], axis=1)], axis=0).astype(BF)
        where = hi_line + jnp.where(lo_line > c.astype(F32), 1.0, 0.0)
        z = jnp.dot((g_id == where).astype(BF), rhs, preferred_element_type=F32)
        for k in range(4):
            tile_ref[k, pl.ds(c, 16, stride=32), :] = z[0:16, k * 128:k * 128 + 128]
            spare[k, pl.ds(pl.multiple_of(c * 8, 8), 8), :] = z[16:24, k * 128:k * 128 + 128]
        return 0

    lax.fori_loop(0, 32, one, 0)
    for k in range(4):
        tail_send[k] = spare[k, pl.ds(0, 32, stride=8), :].astype(BF)


MESH = pl.DeviceIdType.MESH


def whole_kernel(ints_ref, depth_ref, vis_ref, off_ref, scale_ref, beam_ref, meta_ref, place_ref,
                 left_ref, right_ref, stage1_ref, twist_ref, stage2_ref, high_ref, low_ref,
                 dirty_ref, tile_ref,
                 table, zu, mu, zv, wp, sky, box, g_ref, rb, rows_send, rows_recv, scr, lhs, oht, yv, buf, sbuf,
                 high_send, high_recv, spill_send, spill_recv, xh, low_send, low_recv, slot_scr, slot_send, slot_recv,
                 spare, tail_send, tail_recv, sem1, sem2, sem3, sem4, sem5, sem6, sem7, sem8, sem9, local_sem):
    au, me = lax.axis_index("au"), lax.axis_index("vert")
    z, core = me // 2, me % 2
    NZ, NA, NV = 16, 16, 32

    def remote(src, dst, sems, k, to):
        return pltpu.make_async_remote_copy(src_ref=src, dst_ref=dst, send_sem=sems.at[0, k], recv_sem=sems.at[1, k],
                                            device_id=to, device_id_type=MESH)

    def loop(first, last, body):
        lax.fori_loop(first, last, lambda k, _: (body(k), 0)[1], 0)

    barrier = pltpu.get_barrier_semaphore()
    loop(1, NV, lambda k: pl.semaphore_signal(barrier, inc=1, device_id=(au, (me + k) % NV), device_id_type=MESH))
    loop(1, NA, lambda k: pl.semaphore_signal(barrier, inc=1, device_id=((au + k) % NA, me), device_id_type=MESH))

    def spot(core, au, z):
        return (core * NA + au) * NZ + z

    def along_z(k, back):
        peer = (z + NZ - k) % NZ if back else (z + k) % NZ
        return remote(beam_ref.at[0], table.at[spot(core, au, peer if back else z)], sem1, k, (au, peer * 2 + core))

    def over_au(k, back):
        peer = (au + NA - k) % NA if back else (au + k) % NA
        at = table.at[pl.ds(spot(core, peer if back else au, 0), NZ)]
        return remote(at, at, sem2, k, (peer, me))

    def partner(k, back):
        at = table.at[pl.ds(spot(1 - core if back else core, (au + NA - k) % NA, 0), NZ)]
        return remote(at, at, sem3, k, (au, z * 2 + 1 - core))

    own = pltpu.make_async_copy(beam_ref.at[0], table.at[spot(core, au, z)], local_sem.at[0])
    own.start()
    step_setup(vis_ref, off_ref, scale_ref, zu, mu, zv)
    step_sky(0, 3, zu, mu, zv, wp, sky)
    pl.semaphore_wait(barrier, NV - 1 + NA - 1)
    loop(1, NZ, lambda k: along_z(k, False).start())
    step_sky(3, 10, zu, mu, zv, wp, sky)
    own.wait()
    loop(1, NZ, lambda k: along_z(k, True).wait_recv())
    loop(1, NA, lambda k: over_au(k, False).start())
    partner(0, False).start()
    step_sky(10, 12, zu, mu, zv, wp, sky)
    step_screen(ints_ref, depth_ref, sky, box)

    def relay(k):
        over_au(k, True).wait_recv()
        partner(k, False).start()

    loop(1, NA, relay)
    loop(0, NA, lambda k: partner(k, True).wait_recv())
    step_uv(ints_ref, sky, table, meta_ref, left_ref, right_ref, box, g_ref, rb)
    rows_send[...] = rb[...].reshape(32, 16, 128).astype(BF)

    def along_vert(send, recv, sems, k, back):
        peer = (me + NV - k) % NV if back else (me + k) % NV
        return remote(send.at[peer], recv.at[peer if back else me], sems, k, (au, peer))

    def across_au(send, recv, sems, k, back):
        peer = (au + NA - k) % NA if back else (au + k) % NA
        return remote(send.at[peer], recv.at[peer if back else au], sems, k, (peer, me))

    loop(1, NV, lambda k: along_vert(rows_send, rows_recv, sem4, k, False).start())
    rows_recv[me] = rows_send[me]
    step_slots(rb, place_ref, slot_scr, slot_send)
    loop(1, NV, lambda k: along_vert(slot_send, slot_recv, sem5, k, False).start())
    slot_recv[me] = slot_send[me]
    loop(1, NV, lambda k: along_vert(rows_send, rows_recv, sem4, k, True).wait_recv())
    step_rows(me, rows_recv, stage1_ref, twist_ref, stage2_ref, scr, lhs, oht, yv, buf, sbuf, high_send, spill_send)
    loop(1, NA, lambda k: across_au(high_send, high_recv, sem6, k, False).start())
    loop(1, NA, lambda k: across_au(spill_send, spill_recv, sem7, k, False).start())
    high_recv[au] = high_send[au]
    spill_recv[au] = spill_send[au]
    loop(1, NA, lambda k: across_au(high_send, high_recv, sem6, k, True).wait_recv())
    loop(1, NA, lambda k: across_au(spill_send, spill_recv, sem7, k, True).wait_recv())
    step_high(me, high_recv, spill_recv, high_ref, xh, low_send)
    loop(1, NV, lambda k: along_vert(low_send, low_recv, sem8, k, False).start())
    low_recv[me] = low_send[me]
    loop(1, NV, lambda k: along_vert(slot_send, slot_recv, sem5, k, True).wait_recv())
    step_tile(me, scr, slot_recv, slot_scr, spare, tile_ref, tail_send)
    tail = remote(tail_send, tail_recv, sem9, 0, ((au + 1) % NA, me))
    tail.start()
    tail.wait_recv()
    for k in range(4):
        tile_ref[k, 0:32, :] += tail_recv[k].astype(F32)
    loop(1, NV, lambda k: along_vert(low_send, low_recv, sem8, k, True).wait_recv())
    step_low(low_recv, low_ref, buf, dirty_ref)

    loop(1, NZ, lambda k: along_z(k, False).wait_send())
    loop(1, NA, lambda k: over_au(k, False).wait_send())
    loop(0, NA, lambda k: partner(k, False).wait_send())
    loop(1, NV, lambda k: along_vert(rows_send, rows_recv, sem4, k, False).wait_send())
    loop(1, NV, lambda k: along_vert(slot_send, slot_recv, sem5, k, False).wait_send())
    loop(1, NA, lambda k: across_au(high_send, high_recv, sem6, k, False).wait_send())
    loop(1, NA, lambda k: across_au(spill_send, spill_recv, sem7, k, False).wait_send())
    loop(1, NV, lambda k: along_vert(low_send, low_recv, sem8, k, False).wait_send())
    tail.wait_send()


def whole_call(ints, depth, vis, off, scale, beam, meta, place):
    left, right = dft_tables()
    stage1, twist, stage2 = row_tables()
    consts = [jnp.asarray(left, BF), jnp.asarray(right, BF), jnp.asarray(stage1, BF), jnp.asarray(twist, F32),
              jnp.asarray(stage2, BF), jnp.asarray(high_table(), BF), jnp.asarray(low_table(), BF)]
    V, D = pltpu.VMEM, pltpu.SemaphoreType.DMA
    scratch = [
        V((512, 16, 128), BF), V((6, 16, 32, 128), F32), V((8, 16, 32, 128), F32), V((10, 16, 32, 128), F32), V((2, 128, NK), BF),
        V((NS, 64, 32), F32), V((64, 128), F32), V((NS * 64, 32), BF), V((512, 128), F32), V((32, 16, 128), BF), V((32, 16, 128), BF),
        V((512, 128), F32), V((NG * 64, 1536), BF), V((256, 1536), BF), V((NG * 64, 512), F32), V((4, 512, 128), F32), V((256, 128), F32),
        V((16, 32, 512), BF), V((16, 32, 512), BF), V((16, 16, 128), BF), V((16, 16, 128), BF), V((512, 512), BF),
        V((32, 16, 512), BF), V((32, 16, 512), BF), V((1024, 128), F32), V((32, 32, 128), BF), V((32, 32, 128), BF),
        V((4, 256, 128), F32), V((4, 32, 128), BF), V((4, 32, 128), BF),
        D((2, 16)), D((2, 16)), D((2, 16)), D((2, 32)), D((2, 32)), D((2, 16)), D((2, 16)), D((2, 32)), D((2, 1)), D((1,)),
    ]
    return pl.pallas_call(
        whole_kernel,
        out_shape=(jax.ShapeDtypeStruct((16, 64, 256), F32), jax.ShapeDtypeStruct((4, 512, 128), F32)),
        in_specs=[SM] * 2 + [VM] * 13, out_specs=(VM, VM),
        scratch_shapes=scratch,
        compiler_params=pltpu.CompilerParams(collective_id=0, has_side_effects=True, vmem_limit_bytes=60 << 20),
        name="whole",
    )(ints, depth, vis, off, scale, beam, meta, place, *consts)


def on_device(visibilities, baseline_offsets, channel_scale, screen_depth, stations, corners, beam_terms):
    au = lax.axis_index("au")
    row, col = corners[:, 0], corners[:, 1]
    dest = col // 256
    order = jnp.arange(NS, dtype=jnp.int32)
    rank = jnp.sum(((dest[None, :] == dest[:, None]) & (order[None, :] < order[:, None])).astype(jnp.int32), axis=1)
    spots = ((stations & 1) * 16 + stations // 32) * 16 + (stations // 2) % 16
    ints = jnp.stack([row, col, spots[:, 0], spots[:, 1]])
    meta = jnp.pad(jnp.stack([(row - au * 512) // 32, row % 32, col // 32, col % 32]).astype(F32), ((0, 0), (0, 128 - NS)))
    slot = dest + 32 * rank
    gap = jnp.full((4,), -1, jnp.int32)
    slot = jnp.stack([jnp.concatenate([slot[:12], gap, slot[12:], gap]), jnp.concatenate([slot[12:], gap, slot[:12], gap])])
    ids = jnp.arange(64, dtype=jnp.int32)
    place = (jnp.where(ids[:, None] < 32, slot[0][None, :], slot[1][None, :]) == ids[:, None]).astype(BF)
    dirty, tile = whole_call(
        ints, screen_depth,
        visibilities.transpose(1, 0, 2).astype(F32),
        baseline_offsets.transpose(1, 0, 2),
        jnp.broadcast_to(channel_scale[None, :], (128, 16)).reshape(1, NK),
        beam_terms.reshape(1, 16, 128), meta, place,
    )
    gridded = tile.reshape(2, 2, 512, 128).transpose(2, 0, 1, 3).reshape(512, 2, 256)
    return gridded, dirty.reshape(16, 2, 8192)


def solution(mesh):
    from jax.sharding import PartitionSpec as P

    both = ("au", "vert")
    return jax.shard_map(
        on_device,
        mesh=mesh,
        in_specs=(P(both, None, None), P(both, None, None), P(), P(both), P(both, None), P(both, None), P(both, None, None)),
        out_specs=(P("au", None, "vert"), P(both, None, None)),
        check_vma=False,
    )
```

```python
import math
import numpy as np
import jax
import jax.numpy as jnp
from jax import lax
from jax.experimental import pallas as pl
from jax.experimental.pallas import tpu as pltpu

SUB = 32
NS = 24
NK = 2048
F32 = jnp.float32
BF = jnp.bfloat16
VM = pl.BlockSpec(memory_space=pltpu.VMEM)
SM = pl.BlockSpec(memory_space=pltpu.SMEM)


def cmul(ar, ai, br, bi):
    return ar * br - ai * bi, ar * bi + ai * br


def base_phase(theta):
    t = theta * theta
    s = F32(0.0)
    for n in range(17, 1, -2):
        s = (s + F32((-1.0) ** ((n - 1) // 2) / math.factorial(n))) * t
    c = F32(0.0)
    for n in range(18, 0, -2):
        c = (c + F32((-1.0) ** (n // 2) / math.factorial(n))) * t
    return c + F32(1.0), theta * (s + F32(1.0))


def dft_tables():
    x = np.arange(32) - 16
    phi = 2.0 * np.pi / 32 * (x[:, None] * x[None, :] % 32)
    c, s = np.cos(phi) / 32, np.sin(phi) / 32
    left = np.block([[c, s], [-s, c]])
    right = np.concatenate([c, s], axis=1)
    return left.astype(np.float32), right.astype(np.float32)


def phase_table(rows, cols, period):
    phi = 2.0 * np.pi / period * (np.arange(rows)[:, None] * np.arange(cols)[None, :] % period)
    return np.cos(phi), np.sin(phi)


NG = 17


def row_tables():
    c, s = phase_table(256, 256, 256)
    stage1 = np.concatenate([c, s], axis=1)
    twist = np.stack(phase_table(32, 256, 8192))
    c, s = phase_table(32, 32, 32)
    full = np.stack([np.concatenate([c, -s], axis=1), np.concatenate([s, c], axis=1)])
    stage2 = full.reshape(2, 16, 2, 64).transpose(2, 0, 1, 3).reshape(64, 64)
    return stage1, twist, stage2


def high_table():
    c, s = phase_table(256, 256, 256)
    return np.block([[c, s], [-s, c]])


def low_table():
    c, s = phase_table(32, 32, 32)
    return np.block([[c, -s], [s, c]])


def step_setup(vis_ref, off_ref, scale_ref, vs, zu, mu, zv):
    time_id = lax.broadcasted_iota(jnp.int32, (128, NK), 0)
    k_id = lax.broadcasted_iota(jnp.int32, (128, NK), 1)
    spread = (lax.shift_right_logical(k_id, 4) == time_id).astype(F32)
    channel = lax.broadcasted_iota(jnp.int32, (1, NK), 1) & 15
    scale = jnp.zeros((1, NK), F32)
    for c in range(16):
        scale = jnp.where(channel == c, scale_ref[c], scale)
    scale = scale * F32(2.0 * math.pi / SUB)
    vs[...] = vis_ref[...].astype(F32)
    chunks = range(NK // 128)

    def put(dest, n, pair):
        for part in range(2):
            for ch in chunks:
                dest[n + part, ch, 0:NS, :] = pair[part][:, ch * 128:ch * 128 + 128]

    for axis in range(2):
        shift = jnp.dot(off_ref[pl.ds(axis, NS, stride=2), :], spread, precision=lax.Precision.HIGHEST, preferred_element_type=F32)
        e1 = base_phase(shift * scale)
        e2 = cmul(*e1, *e1)
        e4 = cmul(*e2, *e2)
        e8 = cmul(*e4, *e4)
        e16 = cmul(*e8, *e8)
        dest = (zu, zv)[axis]
        put(dest, 0, e1)
        put(dest, 2, e2)
        put(dest, 4, e4)
        if axis == 1:
            put(zv, 6, e8)
            put(zv, 8, e16)
        else:
            for ch in chunks:
                vis = [vs[pl.ds(ch * 2 + part, NS, stride=32), :] for part in range(2)]
                a8 = [x[:, ch * 128:ch * 128 + 128] for x in e8]
                a16 = [x[:, ch * 128:ch * 128 + 128] for x in e16]
                for n, pair in enumerate((cmul(*vis, a16[0], -a16[1]), cmul(*vis, a8[0], -a8[1]), vis, cmul(*vis, *a8))):
                    for part in range(2):
                        mu[2 * n + part, ch, 0:NS, :] = pair[part]


def step_sky(first, last, zu, mu, zv, wp, sky):
    row = lax.broadcasted_iota(jnp.int32, (8, 128), 0)
    bit0, bit1, bit2 = [(lax.shift_right_logical(row, n) & 1) == 1 for n in range(3)]
    one = jnp.ones((8, 128), F32)
    zero = jnp.zeros((8, 128), F32)

    def wide(ref, n, s, chunk):
        return ref[n, chunk, pl.ds(s, 8, stride=0), :]

    def base_tile(ref, s, ch):
        tr = jnp.where(bit0, wide(ref, 0, s, ch), one)
        ti = jnp.where(bit0, wide(ref, 1, s, ch), zero)
        tr, ti = cmul(tr, ti, jnp.where(bit1, wide(ref, 2, s, ch), one), jnp.where(bit1, wide(ref, 3, s, ch), zero))
        return cmul(tr, ti, jnp.where(bit2, wide(ref, 4, s, ch), one), jnp.where(bit2, wide(ref, 5, s, ch), zero))

    def one_subgrid(s, slot):
        for ch in range(NK // 128):
            lo = ch * 128
            br, bi = base_tile(zu, s, ch)
            left = [cmul(br, bi, wide(mu, 2 * n, s, ch), wide(mu, 2 * n + 1, s, ch)) for n in range(4)]
            br, bi = base_tile(zv, s, ch)
            e8r, e8i = wide(zv, 6, s, ch), wide(zv, 7, s, ch)
            e16r, e16i = wide(zv, 8, s, ch), wide(zv, 9, s, ch)
            right = [cmul(br, bi, e16r, -e16i), cmul(br, bi, e8r, -e8i), (br, bi), cmul(br, bi, e8r, e8i)]
            for side, blocks in enumerate((left, right)):
                for part in range(2):
                    for half in range(2):
                        at = side * 64 + part * 32 + half * 16
                        wp[slot, at:at + 16, lo:lo + 128] = jnp.concatenate(
                            [blocks[2 * half][part], blocks[2 * half + 1][part]], axis=0).astype(BF)

    def finish(s, slot):
        prod = lax.dot_general(wp[slot, 0:64, :], wp[slot, 64:128, :], (((1,), (1,)), ((), ())), preferred_element_type=F32)
        sky[s, 0:32, :] = prod[0:32, 0:32] - prod[32:64, 32:64]
        sky[s, 32:64, :] = prod[0:32, 32:64] + prod[32:64, 0:32]

    def pair(i, _):
        one_subgrid(2 * i, 0)
        one_subgrid(2 * i + 1, 1)
        finish(2 * i, 0)
        finish(2 * i + 1, 1)
        return 0

    lax.fori_loop(first, last, pair, 0)


def pixel_ids():
    x = lax.broadcasted_iota(jnp.int32, (8, 128), 0)
    lane = lax.broadcasted_iota(jnp.int32, (8, 128), 1)
    return 4 * x + lax.shift_right_logical(lane, 5) - 16, (lane & 31) - 16


def fold_out(re, im, box, n):
    for y in range(4):
        ra = re if y == 0 else pltpu.roll(re, 128 - 32 * y, 1)
        rb = im if y == 0 else pltpu.roll(im, 128 - 32 * y, 1)
        box[n, pl.ds(y, 8, stride=4), :] = ra
        box[n, pl.ds(32 + y, 8, stride=4), :] = rb


WIDE = 4


def apply_boxes(sky, box, first):
    got = []
    for n in range(WIDE):
        kr, ki = box[n, 0:32, 0:32], box[n, 32:64, 0:32]
        got.append(cmul(sky[first + n, 0:32, :], sky[first + n, 32:64, :], kr, ki))
    return got


def step_screen(corner_ref, depth_ref, sky, box):
    p, q = pixel_ids()
    pf, qf = p.astype(F32), q.astype(F32)
    ap, aq = pf * F32(0.1 / 32), qf * F32(0.1 / 32)
    rad = ap * ap + aq * aq
    tp = (2.0 * pf + 1.0) * F32(1.0 / 32)
    tq = (2.0 * qf + 1.0) * F32(1.0 / 32)
    taper = (1.0 - tp * tp) * (1.0 - tq * tq) * F32(1.0 / math.sqrt(NK))

    def some(i, _):
        for n in range(WIDE):
            s = i * WIDE + n
            turn = (corner_ref[0, s] * p + corner_ref[1, s] * q) & 31
            ang = turn.astype(F32) * F32(2.0 * math.pi / 32) - F32(math.pi) * depth_ref[s] * rad
            fold_out(jnp.cos(ang) * taper, jnp.sin(ang) * taper, box, n)
        for n, pair in enumerate(apply_boxes(sky, box, i * WIDE)):
            sky[i * WIDE + n, 0:32, :] = pair[0]
            sky[i * WIDE + n, 32:64, :] = pair[1]
        return 0

    lax.fori_loop(0, NS // WIDE, some, 0)


def step_notes(au, corner_ref, lines, place):
    lines[...] = jnp.zeros_like(lines)
    lines[0:2, 0:NS] = corner_ref[...]
    row, col = lines[0:1, :], lines[1:2, :]
    dest = lax.shift_right_logical(col, 8)
    across = jnp.broadcast_to(dest.astype(F32), (128, 128))
    down = jnp.transpose(across)
    other = lax.broadcasted_iota(jnp.int32, (128, 128), 0)
    this = lax.broadcasted_iota(jnp.int32, (128, 128), 1)
    earlier = (down == across) & (other < this) & (other < NS)
    rank = jnp.sum(jnp.where(earlier, 1.0, 0.0), axis=0, keepdims=True)
    slot = jnp.where(this[0:1] < NS, dest.astype(F32) + 32.0 * rank, -1.0)
    chosen = (lax.broadcasted_iota(jnp.int32, (64, 128), 0).astype(F32) == slot).astype(BF)
    s = lax.broadcasted_iota(jnp.int32, (128, 32), 0)
    at = lax.broadcasted_iota(jnp.int32, (128, 32), 1)
    y, half = at & 15, lax.shift_right_logical(at, 4)
    for r in range(2):
        pick = (y < 12) & (s == y + 12 * (half if r == 0 else 1 - half))
        place[r * 32:r * 32 + 32, :] = jnp.dot(chosen[r * 32:r * 32 + 32], pick.astype(BF), preferred_element_type=F32).astype(BF)
    lines[0:1, :] = lax.shift_right_arithmetic(row - au * 512, 5)
    lines[1:2, :] = row & 31
    lines[2:3, :] = lax.shift_right_logical(col, 5)
    lines[3:4, :] = col & 31


def step_uv(station_ref, sky, table, lines, left_ref, right_ref, box, g_ref, rb):
    def spot(d):
        return ((d & 1) * 16 + lax.shift_right_logical(d, 5)) * 16 + (lax.shift_right_logical(d, 1) & 15)

    def some(i, _):
        for n in range(WIDE):
            s = i * WIDE + n
            a = table[spot(station_ref[0, s])].astype(F32)
            b = table[spot(station_ref[1, s])].astype(F32)
            pr = a[0:8] * b[0:8] + a[8:16] * b[8:16]
            pi_ = a[8:16] * b[0:8] - a[0:8] * b[8:16]
            fold_out(pr, pi_, box, n)
        for n, pair in enumerate(apply_boxes(sky, box, i * WIDE)):
            cor = jnp.concatenate(pair, axis=0).astype(BF)
            g = jnp.dot(left_ref[...], cor, preferred_element_type=F32)
            g_ref[pl.ds(pl.multiple_of((i * WIDE + n) * 64, 64), 64), :] = g.astype(BF)
        return 0

    lax.fori_loop(0, NS // WIDE, some, 0)

    for y in range(12):
        outs = []
        for half in range(2):
            s = y + 12 * half
            yv = jnp.dot(g_ref[s * 64:s * 64 + 64, :], right_ref[...], preferred_element_type=F32)
            outs.append(yv[0:32, 0:32] + yv[32:64, 32:64])
            outs.append(yv[32:64, 0:32] - yv[0:32, 32:64])
        rb[pl.ds(y, 32, stride=16), :] = jnp.concatenate(outs, axis=1)
    for n in range(4):
        rb[pl.ds(12 + n, 32, stride=16), :] = jnp.broadcast_to(lines[n:n + 1, :], (32, 128)).astype(F32)


def step_slots(rb, place, scr, slot_send):
    low = lax.broadcasted_iota(jnp.int32, (32, 128), 1) < 64

    def some(i, _):
        for n in range(4):
            c = i * 4 + n
            x = rb[pl.ds(pl.multiple_of(c * 16, 16), 16), :]
            both = jnp.concatenate([x, pltpu.roll(x, 64, 1)], axis=0).astype(BF)
            z = jnp.dot(place[...], both, preferred_element_type=F32)
            scr[pl.ds(c, 32, stride=32), :] = jnp.where(low, z[0:32], z[32:64])
        return 0

    lax.fori_loop(0, 8, some, 0)
    slot_send[...] = scr[...].reshape(32, 32, 128).astype(BF)


def step_rows(me, rows_recv, stage1_ref, twist_ref, scr, lhs, oht, yv, turned):
    scr[...] = rows_recv[...].reshape(512, 128).astype(F32)
    lane = lax.broadcasted_iota(jnp.int32, (32, 768), 1)
    src = lax.broadcasted_iota(jnp.int32, (32, 768), 0)
    pick_src = ((lane & 31) == src).astype(BF)
    pick_item = lax.shift_right_logical(lane, 5) == src

    def meta(n):
        table = jnp.transpose(scr[pl.ds(12 + n, 32, stride=16), :])[0:32]
        spread = jnp.dot(table.astype(BF), pick_src, preferred_element_type=F32)
        return jnp.sum(jnp.where(pick_item, spread, 0.0), axis=0, keepdims=True)

    g_hi, g_lo, h, e = [meta(n) for n in range(4)]
    g = g_hi + jnp.where(g_lo > me.astype(F32), 1.0, 0.0)
    h_id = lax.broadcasted_iota(jnp.int32, (256, 768), 0).astype(F32)
    oht[:, 0:768] = (h_id == h).astype(BF)
    oht[:, 768:1536] = (h_id == h + 1.0).astype(BF)
    col = (lax.broadcasted_iota(jnp.int32, (64, 384), 0) & 31).astype(F32)
    for half in range(2):
        parts = []
        for blk in range(3):
            rows = jnp.concatenate([scr[pl.ds(4 * blk + n, 32, stride=16), :] for n in range(4)], axis=0)
            parts.append(jnp.transpose(rows)[half * 64:half * 64 + 64])
        v = jnp.concatenate(parts, axis=1)
        at = half * 384
        first = col >= e[:, at:at + 384]
        hi = jnp.where(first, v, 0.0)
        lo = jnp.where(first, 0.0, v)
        for n in range(NG):
            here = g[:, at:at + 384] == float(n)
            lhs[n * 64:n * 64 + 64, at:at + 384] = jnp.where(here, hi, 0.0).astype(BF)
            lhs[n * 64:n * 64 + 64, 768 + at:768 + at + 384] = jnp.where(here, lo, 0.0).astype(BF)
    x = lax.dot_general(lhs[...], oht[...], (((1,), (1,)), ((), ())), preferred_element_type=F32).astype(BF)
    yv[...] = jnp.dot(x, stage1_ref[...], preferred_element_type=F32)
    for n in range(NG):
        y = yv[n * 64:n * 64 + 64, :]
        re = y[0:32, 0:256] - y[32:64, 256:512]
        im = y[0:32, 256:512] + y[32:64, 0:256]
        re, im = cmul(re, im, twist_ref[0], twist_ref[1])
        turned[n * 64:n * 64 + 64, :] = jnp.concatenate([re, im], axis=0).astype(BF)


def step_split(low, stage2_ref, turned, buf, sbuf, high_send, spill_send):
    for n in range(NG):
        if n == 16 and low == 1:
            continue
        at0, size = (low * 32, 32) if n < 16 else (0, 64)
        z = jnp.dot(stage2_ref[at0:at0 + size, :], turned[n * 64:n * 64 + 64, :], preferred_element_type=F32)
        for at in range(0, size, 16):
            comp = (at // 16) % 2
            for k in range(2):
                piece = z[at:at + 16, k * 128:k * 128 + 128]
                if n < 16:
                    buf[low * 2 + k, pl.ds(comp * 16 + n, 16, stride=32), :] = piece
                else:
                    sbuf[pl.ds(comp * 4 + (at // 32) * 2 + k, 16, stride=16), :] = piece
    for k in range(2):
        high_send[low, :, :, k * 128:k * 128 + 128] = buf[low * 2 + k].reshape(16, 32, 128).astype(BF)
    if low == 0:
        spill_send[...] = sbuf[...].reshape(16, 16, 128).astype(BF)


def step_high(me, low, high_recv, spill_recv, table_ref, xh, low_send):
    first = lax.broadcasted_iota(jnp.int32, (16, 256), 0) == 0
    for r in range(16):
        spill = spill_recv[(r + 15) % 16].astype(F32)
        for comp in range(2):
            block = high_recv[low, r, comp * 16:comp * 16 + 16, :].astype(F32)
            at = comp * 4 + low * 2
            line = jnp.concatenate([spill[at:at + 1], spill[at + 1:at + 2]], axis=1)
            xh[low, comp * 256 + r * 16:comp * 256 + r * 16 + 16, :] = jnp.where(first, block + line, block).astype(BF)
    y = lax.dot_general(xh[low], table_ref[...], (((0,), (0,)), ((), ())), preferred_element_type=F32)
    ql = lax.broadcasted_iota(jnp.int32, (8, 256), 1)
    ang = (ql * me).astype(F32) * F32(2.0 * math.pi / 8192)
    re, im = cmul(y[:, 0:256], y[:, 256:512], jnp.cos(ang)[0:1], jnp.sin(ang)[0:1])
    low_send[low * 16:low * 16 + 16, :, 0:256] = re.reshape(16, 16, 256).astype(BF)
    low_send[low * 16:low * 16 + 16, :, 256:512] = im.reshape(16, 16, 256).astype(BF)


def last_kernel(low_ref, tile_ref, table_ref, dirty_ref, grid_ref, held, scr, sems):
    take = pltpu.make_async_copy(tile_ref, held, sems.at[0])
    take.start()
    for k in range(4):
        scr[k] = low_ref[:, :, k * 128:k * 128 + 128].reshape(512, 128).astype(F32)

    def some(first):
        for m in range(first, first + 8):
            parts = [jnp.concatenate([scr[2 * comp + k, pl.ds(m, 32, stride=16), :] for k in range(2)], axis=1) for comp in range(2)]
            x = jnp.concatenate(parts, axis=0).astype(BF)
            z = jnp.dot(table_ref[...], x, preferred_element_type=F32) * F32(1.0 / (SUB * math.sqrt(12288)))
            for comp in range(2):
                for k in range(2):
                    dirty_ref[m, pl.ds(k * 2 + comp, 32, stride=4), :] = z[comp * 32:comp * 32 + 32, k * 128:k * 128 + 128]

    take.wait()
    give = pltpu.make_async_copy(held, grid_ref, sems.at[1])
    give.start()
    some(0)
    some(8)
    give.wait()


def last_call(low, tile):
    return pl.pallas_call(
        last_kernel,
        out_shape=(jax.ShapeDtypeStruct((16, 128, 128), F32), jax.ShapeDtypeStruct((2048, 128), F32)),
        in_specs=[VM, pl.BlockSpec(memory_space=pl.ANY), VM], out_specs=(VM, pl.BlockSpec(memory_space=pl.ANY)),
        scratch_shapes=[pltpu.VMEM((2048, 128), F32), pltpu.VMEM((4, 512, 128), F32), pltpu.SemaphoreType.DMA((2,))],
        name="last",
    )(low, tile, jnp.asarray(low_table(), BF))


def step_tile(me, scr, slot_recv, vals, spare, tile_ref, tail_send):
    vals[...] = slot_recv[...].reshape(1024, 128).astype(F32)
    hi, lo, h, e = [scr[pl.ds(12 + n, 32, stride=16), :] for n in range(4)]
    lane = lax.broadcasted_iota(jnp.int32, (32, 128), 1)
    base = me.astype(F32) * 8.0
    mine = (h >= base) & (h < base + 8.0) & (lane < NS)
    upto = (lax.broadcasted_iota(jnp.int32, (128, 128), 0) < lax.broadcasted_iota(jnp.int32, (128, 128), 1)).astype(BF)
    order = jnp.dot(mine.astype(BF), upto, preferred_element_type=F32)
    start = (h - base) * 32.0 + e
    column = lax.broadcasted_iota(jnp.int32, (32, 256), 1).astype(F32)
    seen, his, los = [], [], []
    for rank in range(2):
        pick = mine & (order == float(rank))
        hit = jnp.sum(jnp.where(pick, 1.0, 0.0), axis=1, keepdims=True)
        low_edge = jnp.sum(jnp.where(pick, start, 0.0), axis=1, keepdims=True)
        seen.append((column >= low_edge) & (column < low_edge + 32.0 * hit))
        for box, values in ((his, hi), (los, lo)):
            one = jnp.sum(jnp.where(pick, values, 0.0), axis=1, keepdims=True)
            box.append(jnp.transpose(jnp.broadcast_to(one, (32, 128)))[0:1, :])
    hi_line = jnp.concatenate(his, axis=1)
    lo_line = jnp.concatenate(los, axis=1)
    g_id = lax.broadcasted_iota(jnp.int32, (32, 64), 0).astype(F32)
    quarter = lax.shift_right_logical(lane, 5)

    def place_row(c):
        x = vals[pl.ds(c, 32, stride=32), :]
        lines = []
        for rank in range(2):
            for comp in range(2):
                y = jnp.where(quarter == rank * 2 + comp, x, 0.0)
                y = y + pltpu.roll(y, 32, 1)
                y = y + pltpu.roll(y, 64, 1)
                lines.append(jnp.where(seen[rank], jnp.concatenate([y, y], axis=1), 0.0))
        rhs = jnp.concatenate([jnp.concatenate(lines[0:2], axis=1), jnp.concatenate(lines[2:4], axis=1)], axis=0).astype(BF)
        where = hi_line + jnp.where(lo_line > c.astype(F32), 1.0, 0.0)
        z = jnp.dot((g_id == where).astype(BF), rhs, preferred_element_type=F32)
        for comp in range(2):
            for half in range(2):
                at = comp * 2 + half
                tile_ref[pl.ds(c * 4 + half * 2 + comp, 16, stride=128), :] = z[0:16, at * 128:at * 128 + 128]
                spare[at, pl.ds(pl.multiple_of(c * 8, 8), 8), :] = z[16:24, at * 128:at * 128 + 128]

    def some(i, _):
        place_row(i * 2)
        place_row(i * 2 + 1)
        return 0

    lax.fori_loop(0, 16, some, 0)
    for k in range(4):
        tail_send[k] = spare[k, pl.ds(0, 32, stride=8), :].astype(BF)


MESH = pl.DeviceIdType.MESH
SPLIT = 8


def whole_kernel(corner_ref, station_ref, depth_ref, scale_ref, corner_vec, vis_ref, off_ref, beam_ref,
                 left_ref, right_ref, stage1_ref, twist_ref, stage2_ref, high_ref,
                 low_out, tile_out,
                 table, zu, mu, zv, wp, sky, box, g_ref, rb, rows_send, rows_recv, scr, lhs, oht, yv, buf, sbuf,
                 high_send, high_recv, spill_send, spill_recv, xh, low_send, low_recv, slot_scr, slot_send, slot_recv,
                 spare, tail_send, tail_recv, vs, lines, place, own_beam, turned, tile_ref, sem1, sem2, sem3, sem4, sem5, sem6, sem7, sem8, sem9, local_sem):
    au, me = lax.axis_index("au"), lax.axis_index("vert")
    z, core = me // 2, me % 2
    NZ, NA, NV = 16, 16, 32

    def remote(src, dst, sems, k, to):
        return pltpu.make_async_remote_copy(src_ref=src, dst_ref=dst, send_sem=sems.at[0, k], recv_sem=sems.at[1, k],
                                            device_id=to, device_id_type=MESH)

    def loop(first, last, body):
        lax.fori_loop(first, last, lambda k, _: (body(k), 0)[1], 0)

    barrier = pltpu.get_barrier_semaphore()
    loop(1, NV, lambda k: pl.semaphore_signal(barrier, inc=1, device_id=(au, (me + k) % NV), device_id_type=MESH))
    loop(1, NA, lambda k: pl.semaphore_signal(barrier, inc=1, device_id=((au + k) % NA, me), device_id_type=MESH))

    def spot(core, au, z):
        return (core * NA + au) * NZ + z

    def along_z(k, back):
        peer = (z + NZ - k) % NZ if back else (z + k) % NZ
        return remote(own_beam, table.at[spot(core, au, peer if back else z)], sem1, k, (au, peer * 2 + core))

    def over_au(k, back):
        peer = (au + NA - k) % NA if back else (au + k) % NA
        at = table.at[pl.ds(spot(core, peer if back else au, 0), NZ)]
        return remote(at, at, sem2, k, (peer, me))

    def partner(k, back):
        at = table.at[pl.ds(spot(1 - core if back else core, (au + NA - k) % NA, 0), NZ)]
        return remote(at, at, sem3, k, (au, z * 2 + 1 - core))

    box[0, 0:16, :] = beam_ref[...].astype(F32)
    own_beam[...] = jnp.concatenate([box[0, pl.ds(0, 8, stride=2), :], box[0, pl.ds(1, 8, stride=2), :]], axis=0).astype(BF)
    own = pltpu.make_async_copy(own_beam, table.at[spot(core, au, z)], local_sem.at[0])
    own.start()
    pl.semaphore_wait(barrier, NV - 1 + NA - 1)
    loop(1, NZ, lambda k: along_z(k, False).start())
    step_setup(vis_ref, off_ref, scale_ref, vs, zu, mu, zv)
    step_sky(0, SPLIT, zu, mu, zv, wp, sky)
    own.wait()
    loop(1, NZ, lambda k: along_z(k, True).wait_recv())
    loop(1, NA, lambda k: over_au(k, False).start())
    partner(0, False).start()
    step_sky(SPLIT, 12, zu, mu, zv, wp, sky)
    step_notes(au, corner_vec, lines, place)
    step_screen(corner_ref, depth_ref, sky, box)

    def relay(k):
        over_au(k, True).wait_recv()
        partner(k, False).start()

    loop(1, NA, relay)
    loop(0, NA, lambda k: partner(k, True).wait_recv())
    step_uv(station_ref, sky, table, lines, left_ref, right_ref, box, g_ref, rb)
    rows_send[...] = rb[...].reshape(32, 16, 128).astype(BF)

    def along_vert(send, recv, sems, k, back):
        peer = (me + NV - k) % NV if back else (me + k) % NV
        return remote(send.at[peer], recv.at[peer if back else me], sems, k, (au, peer))

    def across_au(send, recv, sems, k, back):
        peer = (au + NA - k) % NA if back else (au + k) % NA
        return remote(send.at[peer], recv.at[peer if back else au], sems, k, (peer, me))

    loop(1, NV, lambda k: along_vert(rows_send, rows_recv, sem4, k, False).start())
    rows_recv[me] = rows_send[me]
    step_slots(rb, place, slot_scr, slot_send)
    loop(1, NV, lambda k: along_vert(slot_send, slot_recv, sem5, k, False).start())
    slot_recv[me] = slot_send[me]
    loop(1, NV, lambda k: along_vert(rows_send, rows_recv, sem4, k, True).wait_recv())
    step_rows(me, rows_recv, stage1_ref, twist_ref, scr, lhs, oht, yv, turned)

    def half_across(low, k, back):
        peer = (au + NA - k) % NA if back else (au + k) % NA
        return remote(high_send.at[low, peer], high_recv.at[low, peer if back else au], sem6, low * NA + k, (peer, me))

    for low in range(2):
        step_split(low, stage2_ref, turned, buf, sbuf, high_send, spill_send)
        loop(1, NA, lambda k: half_across(low, k, False).start())
        high_recv[low, au] = high_send[low, au]
        if low == 0:
            loop(1, NA, lambda k: across_au(spill_send, spill_recv, sem7, k, False).start())
            spill_recv[au] = spill_send[au]
    loop(1, NA, lambda k: across_au(spill_send, spill_recv, sem7, k, True).wait_recv())
    for low in range(2):
        loop(1, NA, lambda k: half_across(low, k, True).wait_recv())
        step_high(me, low, high_recv, spill_recv, high_ref, xh, low_send)

        def send_low(k):
            @pl.when(((me + k) % NV) // 16 == low)
            def _():
                along_vert(low_send, low_recv, sem8, k, False).start()

        loop(1, NV, send_low)
    low_recv[me] = low_send[me]
    loop(1, NV, lambda k: along_vert(slot_send, slot_recv, sem5, k, True).wait_recv())
    step_tile(me, scr, slot_recv, slot_scr, spare, tile_ref, tail_send)
    tail = remote(tail_send, tail_recv, sem9, 0, ((au + 1) % NA, me))
    tail.start()
    tail.wait_recv()
    for k in range(4):
        tile_ref[pl.ds((k % 2) * 2 + k // 2, 32, stride=4), :] += tail_recv[k].astype(F32)
    put_tile = pltpu.make_async_copy(tile_ref, tile_out, local_sem.at[1])
    put_tile.start()
    loop(1, NV, lambda k: along_vert(low_send, low_recv, sem8, k, True).wait_recv())
    put_low = pltpu.make_async_copy(low_recv, low_out, local_sem.at[2])
    put_low.start()

    loop(1, NZ, lambda k: along_z(k, False).wait_send())
    loop(1, NA, lambda k: over_au(k, False).wait_send())
    loop(0, NA, lambda k: partner(k, False).wait_send())
    loop(1, NV, lambda k: along_vert(rows_send, rows_recv, sem4, k, False).wait_send())
    loop(1, NV, lambda k: along_vert(slot_send, slot_recv, sem5, k, False).wait_send())
    for low in range(2):
        loop(1, NA, lambda k: half_across(low, k, False).wait_send())
    loop(1, NA, lambda k: across_au(spill_send, spill_recv, sem7, k, False).wait_send())
    loop(1, NV, lambda k: along_vert(low_send, low_recv, sem8, k, False).wait_send())
    tail.wait_send()
    put_tile.wait()
    put_low.wait()


def whole_call(corners, stations, depth, scale, vis, off, beam):
    left, right = dft_tables()
    stage1, twist, stage2 = row_tables()
    consts = [jnp.asarray(left, BF), jnp.asarray(right, BF), jnp.asarray(stage1, BF), jnp.asarray(twist, F32),
              jnp.asarray(stage2, BF), jnp.asarray(high_table(), BF)]
    V, D = pltpu.VMEM, pltpu.SemaphoreType.DMA
    scratch = [
        V((512, 16, 128), BF), V((6, 16, 32, 128), F32), V((8, 16, 32, 128), F32), V((10, 16, 32, 128), F32), V((2, 128, NK), BF),
        V((NS, 64, 32), F32), V((WIDE, 64, 128), F32), V((NS * 64, 32), BF), V((512, 128), F32), V((32, 16, 128), BF), V((32, 16, 128), BF),
        V((512, 128), F32), V((NG * 64, 1536), BF), V((256, 1536), BF), V((NG * 64, 512), F32), V((4, 512, 128), F32), V((256, 128), F32),
        V((2, 16, 32, 256), BF), V((2, 16, 32, 256), BF), V((16, 16, 128), BF), V((16, 16, 128), BF), V((2, 512, 256), BF),
        V((32, 16, 512), BF), V((32, 16, 512), BF), V((1024, 128), F32), V((32, 32, 128), BF), V((32, 32, 128), BF),
        V((4, 256, 128), F32), V((4, 32, 128), BF), V((4, 32, 128), BF),
        V((768, 128), F32), V((8, 128), jnp.int32), V((64, 32), BF), V((16, 128), BF), V((NG * 64, 256), BF), V((2048, 128), F32),
        D((2, 16)), D((2, 16)), D((2, 16)), D((2, 32)), D((2, 32)), D((2, 32)), D((2, 16)), D((2, 32)), D((2, 1)), D((3,)),
    ]
    return pl.pallas_call(
        whole_kernel,
        out_shape=(jax.ShapeDtypeStruct((32, 16, 512), BF), jax.ShapeDtypeStruct((2048, 128), F32)),
        in_specs=[SM] * 4 + [VM] * 10, out_specs=(pl.BlockSpec(memory_space=pl.ANY),) * 2,
        scratch_shapes=scratch,
        compiler_params=pltpu.CompilerParams(collective_id=0, has_side_effects=True, vmem_limit_bytes=60 << 20),
        name="whole",
    )(corners, stations, depth, scale, corners, vis, off, beam, *consts)


def on_device(visibilities, baseline_offsets, channel_scale, screen_depth, stations, corners, beam_terms):
    low, tile = whole_call(
        corners.T, stations.T, screen_depth, channel_scale,
        visibilities.reshape(NS, 2, 16, 128).transpose(0, 2, 1, 3).reshape(768, 128),
        baseline_offsets.reshape(48, 128),
        beam_terms.reshape(2, 8, 128).transpose(1, 0, 2).reshape(16, 128),
    )
    dirty, tile = last_call(low, tile)
    gridded = tile.reshape(512, 2, 2, 128).transpose(0, 2, 1, 3).reshape(512, 2, 256)
    return gridded, dirty.reshape(16, 64, 2, 128).transpose(0, 2, 1, 3).reshape(16, 2, 8192)


def solution(mesh):
    from jax.sharding import PartitionSpec as P

    both = ("au", "vert")
    return jax.shard_map(
        on_device,
        mesh=mesh,
        in_specs=(P(both, None, None), P(both, None, None), P(), P(both), P(both, None), P(both, None), P(both, None, None)),
        out_specs=(P("au", None, "vert"), P(both, None, None)),
        check_vma=False,
    )
```

```python
import math
import numpy as np
import jax
import jax.numpy as jnp
from jax import lax
from jax.experimental import pallas as pl
from jax.experimental.pallas import tpu as pltpu

SUB = 32
NS = 24
NK = 2048
F32 = jnp.float32
BF = jnp.bfloat16
VM = pl.BlockSpec(memory_space=pltpu.VMEM)
SM = pl.BlockSpec(memory_space=pltpu.SMEM)


def cmul(ar, ai, br, bi):
    return ar * br - ai * bi, ar * bi + ai * br


def base_phase(theta):
    t = theta * theta
    s = F32(0.0)
    for n in range(17, 1, -2):
        s = (s + F32((-1.0) ** ((n - 1) // 2) / math.factorial(n))) * t
    c = F32(0.0)
    for n in range(18, 0, -2):
        c = (c + F32((-1.0) ** (n // 2) / math.factorial(n))) * t
    return c + F32(1.0), theta * (s + F32(1.0))


def dft_tables():
    x = np.arange(32) - 16
    phi = 2.0 * np.pi / 32 * (x[:, None] * x[None, :] % 32)
    c, s = np.cos(phi) / 32, np.sin(phi) / 32
    left = np.block([[c, s], [-s, c]])
    right = np.concatenate([c, s], axis=1)
    return left.astype(np.float32), right.astype(np.float32)


def phase_table(rows, cols, period):
    phi = 2.0 * np.pi / period * (np.arange(rows)[:, None] * np.arange(cols)[None, :] % period)
    return np.cos(phi), np.sin(phi)


NG = 17


def row_tables():
    c, s = phase_table(256, 256, 256)
    stage1 = np.concatenate([c, s], axis=1)
    twist = np.stack(phase_table(32, 256, 8192))
    c, s = phase_table(32, 32, 32)
    full = np.stack([np.concatenate([c, -s], axis=1), np.concatenate([s, c], axis=1)])
    stage2 = full.reshape(2, 16, 2, 64).transpose(2, 0, 1, 3).reshape(64, 64)
    return stage1, twist, stage2


def high_table():
    c, s = phase_table(256, 256, 256)
    return np.block([[c, s], [-s, c]])


def low_table():
    c, s = phase_table(32, 32, 32)
    return np.block([[c, -s], [s, c]])


def step_setup(vis_ref, off_ref, scale_ref, vs, zu, mu, zv):
    time_id = lax.broadcasted_iota(jnp.int32, (128, NK), 0)
    k_id = lax.broadcasted_iota(jnp.int32, (128, NK), 1)
    spread = (lax.shift_right_logical(k_id, 4) == time_id).astype(F32)
    channel = lax.broadcasted_iota(jnp.int32, (1, NK), 1) & 15
    scale = jnp.zeros((1, NK), F32)
    for c in range(16):
        scale = jnp.where(channel == c, scale_ref[c], scale)
    scale = scale * F32(2.0 * math.pi / SUB)
    vs[...] = vis_ref[...].astype(F32)
    chunks = range(NK // 128)

    def put(dest, n, pair):
        for part in range(2):
            for ch in chunks:
                dest[n + part, ch, 0:NS, :] = pair[part][:, ch * 128:ch * 128 + 128]

    for axis in range(2):
        shift = jnp.dot(off_ref[pl.ds(axis, NS, stride=2), :], spread, precision=lax.Precision.HIGHEST, preferred_element_type=F32)
        e1 = base_phase(shift * scale)
        e2 = cmul(*e1, *e1)
        e4 = cmul(*e2, *e2)
        e8 = cmul(*e4, *e4)
        e16 = cmul(*e8, *e8)
        dest = (zu, zv)[axis]
        put(dest, 0, e1)
        put(dest, 2, e2)
        put(dest, 4, e4)
        if axis == 1:
            put(zv, 6, e8)
            put(zv, 8, e16)
        else:
            for ch in chunks:
                vis = [vs[pl.ds(ch * 2 + part, NS, stride=32), :] for part in range(2)]
                a8 = [x[:, ch * 128:ch * 128 + 128] for x in e8]
                a16 = [x[:, ch * 128:ch * 128 + 128] for x in e16]
                for n, pair in enumerate((cmul(*vis, a16[0], -a16[1]), cmul(*vis, a8[0], -a8[1]), vis, cmul(*vis, *a8))):
                    for part in range(2):
                        mu[2 * n + part, ch, 0:NS, :] = pair[part]


def step_sky(first, last, zu, mu, zv, wp, sky):
    row = lax.broadcasted_iota(jnp.int32, (8, 128), 0)
    bit0, bit1, bit2 = [(lax.shift_right_logical(row, n) & 1) == 1 for n in range(3)]
    one = jnp.ones((8, 128), F32)
    zero = jnp.zeros((8, 128), F32)

    def wide(ref, n, s, chunk):
        return ref[n, chunk, pl.ds(s, 8, stride=0), :]

    def base_tile(ref, s, ch):
        tr = jnp.where(bit0, wide(ref, 0, s, ch), one)
        ti = jnp.where(bit0, wide(ref, 1, s, ch), zero)
        tr, ti = cmul(tr, ti, jnp.where(bit1, wide(ref, 2, s, ch), one), jnp.where(bit1, wide(ref, 3, s, ch), zero))
        return cmul(tr, ti, jnp.where(bit2, wide(ref, 4, s, ch), one), jnp.where(bit2, wide(ref, 5, s, ch), zero))

    def one_subgrid(s, slot):
        for ch in range(NK // 128):
            lo = ch * 128
            br, bi = base_tile(zu, s, ch)
            left = [cmul(br, bi, wide(mu, 2 * n, s, ch), wide(mu, 2 * n + 1, s, ch)) for n in range(4)]
            br, bi = base_tile(zv, s, ch)
            e8r, e8i = wide(zv, 6, s, ch), wide(zv, 7, s, ch)
            e16r, e16i = wide(zv, 8, s, ch), wide(zv, 9, s, ch)
            right = [cmul(br, bi, e16r, -e16i), cmul(br, bi, e8r, -e8i), (br, bi), cmul(br, bi, e8r, e8i)]
            for side, blocks in enumerate((left, right)):
                for part in range(2):
                    for half in range(2):
                        at = side * 64 + part * 32 + half * 16
                        wp[slot, at:at + 16, lo:lo + 128] = jnp.concatenate(
                            [blocks[2 * half][part], blocks[2 * half + 1][part]], axis=0).astype(BF)

    def finish(s, slot):
        prod = lax.dot_general(wp[slot, 0:64, :], wp[slot, 64:128, :], (((1,), (1,)), ((), ())), preferred_element_type=F32)
        sky[s, 0:32, :] = prod[0:32, 0:32] - prod[32:64, 32:64]
        sky[s, 32:64, :] = prod[0:32, 32:64] + prod[32:64, 0:32]

    def pair(i, _):
        one_subgrid(2 * i, 0)
        one_subgrid(2 * i + 1, 1)
        finish(2 * i, 0)
        finish(2 * i + 1, 1)
        return 0

    lax.fori_loop(first, last, pair, 0)


def pixel_ids():
    x = lax.broadcasted_iota(jnp.int32, (8, 128), 0)
    lane = lax.broadcasted_iota(jnp.int32, (8, 128), 1)
    return 4 * x + lax.shift_right_logical(lane, 5) - 16, (lane & 31) - 16


def fold_out(re, im, box, n):
    for y in range(4):
        ra = re if y == 0 else pltpu.roll(re, 128 - 32 * y, 1)
        rb = im if y == 0 else pltpu.roll(im, 128 - 32 * y, 1)
        box[n, pl.ds(y, 8, stride=4), :] = ra
        box[n, pl.ds(32 + y, 8, stride=4), :] = rb


WIDE = 4


def apply_boxes(sky, box, first):
    got = []
    for n in range(WIDE):
        kr, ki = box[n, 0:32, 0:32], box[n, 32:64, 0:32]
        got.append(cmul(sky[first + n, 0:32, :], sky[first + n, 32:64, :], kr, ki))
    return got


def step_screen(corner_ref, depth_ref, sky, box):
    p, q = pixel_ids()
    pf, qf = p.astype(F32), q.astype(F32)
    ap, aq = pf * F32(0.1 / 32), qf * F32(0.1 / 32)
    rad = ap * ap + aq * aq
    tp = (2.0 * pf + 1.0) * F32(1.0 / 32)
    tq = (2.0 * qf + 1.0) * F32(1.0 / 32)
    taper = (1.0 - tp * tp) * (1.0 - tq * tq) * F32(1.0 / math.sqrt(NK))

    def some(i, _):
        for n in range(WIDE):
            s = i * WIDE + n
            turn = (corner_ref[0, s] * p + corner_ref[1, s] * q) & 31
            ang = turn.astype(F32) * F32(2.0 * math.pi / 32) - F32(math.pi) * depth_ref[s] * rad
            fold_out(jnp.cos(ang) * taper, jnp.sin(ang) * taper, box, n)
        for n, pair in enumerate(apply_boxes(sky, box, i * WIDE)):
            sky[i * WIDE + n, 0:32, :] = pair[0]
            sky[i * WIDE + n, 32:64, :] = pair[1]
        return 0

    lax.fori_loop(0, NS // WIDE, some, 0)


def step_notes(au, corner_ref, lines, place):
    lines[...] = jnp.zeros_like(lines)
    lines[0:2, 0:NS] = corner_ref[...]
    row, col = lines[0:1, :], lines[1:2, :]
    dest = lax.shift_right_logical(col, 8)
    across = jnp.broadcast_to(dest.astype(F32), (128, 128))
    down = jnp.transpose(across)
    other = lax.broadcasted_iota(jnp.int32, (128, 128), 0)
    this = lax.broadcasted_iota(jnp.int32, (128, 128), 1)
    earlier = (down == across) & (other < this) & (other < NS)
    rank = jnp.sum(jnp.where(earlier, 1.0, 0.0), axis=0, keepdims=True)
    slot = jnp.where(this[0:1] < NS, dest.astype(F32) + 32.0 * rank, -1.0)
    chosen = (lax.broadcasted_iota(jnp.int32, (64, 128), 0).astype(F32) == slot).astype(BF)
    s = lax.broadcasted_iota(jnp.int32, (128, 32), 0)
    at = lax.broadcasted_iota(jnp.int32, (128, 32), 1)
    y, half = at & 15, lax.shift_right_logical(at, 4)
    for r in range(2):
        pick = (y < 12) & (s == y + 12 * (half if r == 0 else 1 - half))
        place[r * 32:r * 32 + 32, :] = jnp.dot(chosen[r * 32:r * 32 + 32], pick.astype(BF), preferred_element_type=F32).astype(BF)
    lines[0:1, :] = lax.shift_right_arithmetic(row - au * 512, 5)
    lines[1:2, :] = row & 31
    lines[2:3, :] = lax.shift_right_logical(col, 5)
    lines[3:4, :] = col & 31


def step_uv(station_ref, sky, table, lines, left_ref, right_ref, box, g_ref, rb):
    def beam(d):
        return table[d & 1, lax.shift_right_logical(d, 7), lax.shift_right_logical(d, 5) & 3, lax.shift_right_logical(d, 1) & 15].astype(F32)

    def some(i, _):
        for n in range(WIDE):
            s = i * WIDE + n
            a = beam(station_ref[0, s])
            b = beam(station_ref[1, s])
            pr = a[0:8] * b[0:8] + a[8:16] * b[8:16]
            pi_ = a[8:16] * b[0:8] - a[0:8] * b[8:16]
            fold_out(pr, pi_, box, n)
        for n, pair in enumerate(apply_boxes(sky, box, i * WIDE)):
            cor = jnp.concatenate(pair, axis=0).astype(BF)
            g = jnp.dot(left_ref[...], cor, preferred_element_type=F32)
            g_ref[pl.ds(pl.multiple_of((i * WIDE + n) * 64, 64), 64), :] = g.astype(BF)
        return 0

    lax.fori_loop(0, NS // WIDE, some, 0)

    for y in range(12):
        outs = []
        for half in range(2):
            s = y + 12 * half
            yv = jnp.dot(g_ref[s * 64:s * 64 + 64, :], right_ref[...], preferred_element_type=F32)
            outs.append(yv[0:32, 0:32] + yv[32:64, 32:64])
            outs.append(yv[32:64, 0:32] - yv[0:32, 32:64])
        rb[pl.ds(y, 32, stride=16), :] = jnp.concatenate(outs, axis=1)
    for n in range(4):
        rb[pl.ds(12 + n, 32, stride=16), :] = jnp.broadcast_to(lines[n:n + 1, :], (32, 128)).astype(F32)


def step_slots(rb, place, scr, slot_send):
    low = lax.broadcasted_iota(jnp.int32, (32, 128), 1) < 64

    def some(i, _):
        for n in range(4):
            c = i * 4 + n
            x = rb[pl.ds(pl.multiple_of(c * 16, 16), 16), :]
            both = jnp.concatenate([x, pltpu.roll(x, 64, 1)], axis=0).astype(BF)
            z = jnp.dot(place[...], both, preferred_element_type=F32)
            scr[pl.ds(c, 32, stride=32), :] = jnp.where(low, z[0:32], z[32:64])
        return 0

    lax.fori_loop(0, 8, some, 0)
    slot_send[...] = scr[...].reshape(32, 32, 128).astype(BF)


def step_rows(me, rows_recv, stage1_ref, twist_ref, scr, lhs, oht, yv, turned):
    scr[...] = rows_recv[...].reshape(512, 128).astype(F32)
    lane = lax.broadcasted_iota(jnp.int32, (32, 768), 1)
    src = lax.broadcasted_iota(jnp.int32, (32, 768), 0)
    pick_src = ((lane & 31) == src).astype(BF)
    pick_item = lax.shift_right_logical(lane, 5) == src

    def meta(n):
        table = jnp.transpose(scr[pl.ds(12 + n, 32, stride=16), :])[0:32]
        spread = jnp.dot(table.astype(BF), pick_src, preferred_element_type=F32)
        return jnp.sum(jnp.where(pick_item, spread, 0.0), axis=0, keepdims=True)

    g_hi, g_lo, h, e = [meta(n) for n in range(4)]
    g = g_hi + jnp.where(g_lo > me.astype(F32), 1.0, 0.0)
    h_id = lax.broadcasted_iota(jnp.int32, (256, 768), 0).astype(F32)
    oht[:, 0:768] = (h_id == h).astype(BF)
    oht[:, 768:1536] = (h_id == h + 1.0).astype(BF)
    col = (lax.broadcasted_iota(jnp.int32, (64, 384), 0) & 31).astype(F32)
    for half in range(2):
        parts = []
        for blk in range(3):
            rows = jnp.concatenate([scr[pl.ds(4 * blk + n, 32, stride=16), :] for n in range(4)], axis=0)
            parts.append(jnp.transpose(rows)[half * 64:half * 64 + 64])
        v = jnp.concatenate(parts, axis=1)
        at = half * 384
        first = col >= e[:, at:at + 384]
        hi = jnp.where(first, v, 0.0)
        lo = jnp.where(first, 0.0, v)
        for n in range(NG):
            here = g[:, at:at + 384] == float(n)
            lhs[n * 64:n * 64 + 64, at:at + 384] = jnp.where(here, hi, 0.0).astype(BF)
            lhs[n * 64:n * 64 + 64, 768 + at:768 + at + 384] = jnp.where(here, lo, 0.0).astype(BF)
    x = lax.dot_general(lhs[...], oht[...], (((1,), (1,)), ((), ())), preferred_element_type=F32).astype(BF)
    yv[...] = jnp.dot(x, stage1_ref[...], preferred_element_type=F32)
    for n in range(NG):
        y = yv[n * 64:n * 64 + 64, :]
        re = y[0:32, 0:256] - y[32:64, 256:512]
        im = y[0:32, 256:512] + y[32:64, 0:256]
        re, im = cmul(re, im, twist_ref[0], twist_ref[1])
        turned[n * 64:n * 64 + 64, :] = jnp.concatenate([re, im], axis=0).astype(BF)


def step_split(low, stage2_ref, turned, buf, sbuf, high_send, spill_send):
    for n in range(NG):
        if n == 16 and low == 1:
            continue
        at0, size = (low * 32, 32) if n < 16 else (0, 64)
        z = jnp.dot(stage2_ref[at0:at0 + size, :], turned[n * 64:n * 64 + 64, :], preferred_element_type=F32)
        for at in range(0, size, 16):
            comp = (at // 16) % 2
            for k in range(2):
                piece = z[at:at + 16, k * 128:k * 128 + 128]
                if n < 16:
                    buf[low * 2 + k, pl.ds(comp * 16 + n, 16, stride=32), :] = piece
                else:
                    sbuf[pl.ds(comp * 4 + (at // 32) * 2 + k, 16, stride=16), :] = piece
    for k in range(2):
        high_send[low, :, :, k * 128:k * 128 + 128] = buf[low * 2 + k].reshape(16, 32, 128).astype(BF)
    if low == 0:
        spill_send[...] = sbuf[...].reshape(16, 16, 128).astype(BF)


def step_high(me, low, high_recv, spill_recv, table_ref, xh, low_send):
    first = lax.broadcasted_iota(jnp.int32, (16, 256), 0) == 0
    for r in range(16):
        spill = spill_recv[(r + 15) % 16].astype(F32)
        for comp in range(2):
            block = high_recv[low, r, comp * 16:comp * 16 + 16, :].astype(F32)
            at = comp * 4 + low * 2
            line = jnp.concatenate([spill[at:at + 1], spill[at + 1:at + 2]], axis=1)
            xh[low, comp * 256 + r * 16:comp * 256 + r * 16 + 16, :] = jnp.where(first, block + line, block).astype(BF)
    y = lax.dot_general(xh[low], table_ref[...], (((0,), (0,)), ((), ())), preferred_element_type=F32)
    ql = lax.broadcasted_iota(jnp.int32, (8, 256), 1)
    ang = (ql * me).astype(F32) * F32(2.0 * math.pi / 8192)
    re, im = cmul(y[:, 0:256], y[:, 256:512], jnp.cos(ang)[0:1], jnp.sin(ang)[0:1])
    low_send[low * 16:low * 16 + 16, :, 0:256] = re.reshape(16, 16, 256).astype(BF)
    low_send[low * 16:low * 16 + 16, :, 256:512] = im.reshape(16, 16, 256).astype(BF)


def last_kernel(low_ref, tile_ref, table_ref, dirty_ref, grid_ref, held, scr, sems):
    take = pltpu.make_async_copy(tile_ref, held, sems.at[0])
    take.start()
    for k in range(4):
        scr[k] = low_ref[:, :, k * 128:k * 128 + 128].reshape(512, 128).astype(F32)

    def some(first):
        for m in range(first, first + 8):
            parts = [jnp.concatenate([scr[2 * comp + k, pl.ds(m, 32, stride=16), :] for k in range(2)], axis=1) for comp in range(2)]
            x = jnp.concatenate(parts, axis=0).astype(BF)
            z = jnp.dot(table_ref[...], x, preferred_element_type=F32) * F32(1.0 / (SUB * math.sqrt(12288)))
            for comp in range(2):
                for k in range(2):
                    dirty_ref[m, pl.ds(k * 2 + comp, 32, stride=4), :] = z[comp * 32:comp * 32 + 32, k * 128:k * 128 + 128]

    take.wait()
    give = pltpu.make_async_copy(held, grid_ref, sems.at[1])
    give.start()
    some(0)
    some(8)
    give.wait()


def last_call(low, tile):
    return pl.pallas_call(
        last_kernel,
        out_shape=(jax.ShapeDtypeStruct((16, 128, 128), F32), jax.ShapeDtypeStruct((2048, 128), F32)),
        in_specs=[VM, pl.BlockSpec(memory_space=pl.ANY), VM], out_specs=(VM, pl.BlockSpec(memory_space=pl.ANY)),
        scratch_shapes=[pltpu.VMEM((2048, 128), F32), pltpu.VMEM((4, 512, 128), F32), pltpu.SemaphoreType.DMA((2,))],
        name="last",
    )(low, tile, jnp.asarray(low_table(), BF))


def step_tile(me, scr, slot_recv, vals, spare, tile_ref, tail_send):
    vals[...] = slot_recv[...].reshape(1024, 128).astype(F32)
    hi, lo, h, e = [scr[pl.ds(12 + n, 32, stride=16), :] for n in range(4)]
    lane = lax.broadcasted_iota(jnp.int32, (32, 128), 1)
    base = me.astype(F32) * 8.0
    mine = (h >= base) & (h < base + 8.0) & (lane < NS)
    upto = (lax.broadcasted_iota(jnp.int32, (128, 128), 0) < lax.broadcasted_iota(jnp.int32, (128, 128), 1)).astype(BF)
    order = jnp.dot(mine.astype(BF), upto, preferred_element_type=F32)
    start = (h - base) * 32.0 + e
    column = lax.broadcasted_iota(jnp.int32, (32, 256), 1).astype(F32)
    seen, his, los = [], [], []
    for rank in range(2):
        pick = mine & (order == float(rank))
        hit = jnp.sum(jnp.where(pick, 1.0, 0.0), axis=1, keepdims=True)
        low_edge = jnp.sum(jnp.where(pick, start, 0.0), axis=1, keepdims=True)
        seen.append((column >= low_edge) & (column < low_edge + 32.0 * hit))
        for box, values in ((his, hi), (los, lo)):
            one = jnp.sum(jnp.where(pick, values, 0.0), axis=1, keepdims=True)
            box.append(jnp.transpose(jnp.broadcast_to(one, (32, 128)))[0:1, :])
    hi_line = jnp.concatenate(his, axis=1)
    lo_line = jnp.concatenate(los, axis=1)
    g_id = lax.broadcasted_iota(jnp.int32, (32, 64), 0).astype(F32)
    quarter = lax.shift_right_logical(lane, 5)

    def place_row(c):
        x = vals[pl.ds(c, 32, stride=32), :]
        lines = []
        for rank in range(2):
            for comp in range(2):
                y = jnp.where(quarter == rank * 2 + comp, x, 0.0)
                y = y + pltpu.roll(y, 32, 1)
                y = y + pltpu.roll(y, 64, 1)
                lines.append(jnp.where(seen[rank], jnp.concatenate([y, y], axis=1), 0.0))
        rhs = jnp.concatenate([jnp.concatenate(lines[0:2], axis=1), jnp.concatenate(lines[2:4], axis=1)], axis=0).astype(BF)
        where = hi_line + jnp.where(lo_line > c.astype(F32), 1.0, 0.0)
        z = jnp.dot((g_id == where).astype(BF), rhs, preferred_element_type=F32)
        for comp in range(2):
            for half in range(2):
                at = comp * 2 + half
                tile_ref[pl.ds(c * 4 + half * 2 + comp, 16, stride=128), :] = z[0:16, at * 128:at * 128 + 128]
                spare[at, pl.ds(pl.multiple_of(c * 8, 8), 8), :] = z[16:24, at * 128:at * 128 + 128]

    def some(i, _):
        place_row(i * 2)
        place_row(i * 2 + 1)
        return 0

    lax.fori_loop(0, 16, some, 0)
    for k in range(4):
        tail_send[k] = spare[k, pl.ds(0, 32, stride=8), :].astype(BF)


MESH = pl.DeviceIdType.MESH
SPLIT = 8


def whole_kernel(corner_ref, station_ref, depth_ref, scale_ref, corner_vec, vis_ref, off_ref, beam_ref,
                 left_ref, right_ref, stage1_ref, twist_ref, stage2_ref, high_ref,
                 low_out, tile_out,
                 table, zu, mu, zv, wp, sky, box, g_ref, rb, rows_send, rows_recv, scr, lhs, oht, yv, buf, sbuf,
                 high_send, high_recv, spill_send, spill_recv, xh, low_send, low_recv, slot_scr, slot_send, slot_recv,
                 spare, tail_send, tail_recv, vs, lines, place, own_beam, turned, tile_ref, sem1, sem2, sem3, sem4, sem5, sem6, sem7, sem8, sem9, local_sem):
    au, me = lax.axis_index("au"), lax.axis_index("vert")
    z, core = me // 2, me % 2
    NZ, NA, NV = 16, 16, 32

    def remote(src, dst, sems, k, to):
        return pltpu.make_async_remote_copy(src_ref=src, dst_ref=dst, send_sem=sems.at[0, k], recv_sem=sems.at[1, k],
                                            device_id=to, device_id_type=MESH)

    def loop(first, last, body):
        lax.fori_loop(first, last, lambda k, _: (body(k), 0)[1], 0)

    barrier = pltpu.get_barrier_semaphore()
    loop(1, NV, lambda k: pl.semaphore_signal(barrier, inc=1, device_id=(au, (me + k) % NV), device_id_type=MESH))
    loop(1, NA, lambda k: pl.semaphore_signal(barrier, inc=1, device_id=((au + k) % NA, me), device_id_type=MESH))

    y, x = au // 4, au % 4

    def less(a, k):
        return (a + 4 - k) % 4

    def along_z(k, back):
        peer = (z + NZ - k) % NZ if back else (z + k) % NZ
        return remote(own_beam, table.at[core, y, x, peer if back else z], sem1, k, (au, peer * 2 + core))

    def over_x(k, back):
        at = table.at[core, y, less(x, k) if back else x]
        return remote(at, at, sem2, k, (y * 4 + (x + k) % 4, me))

    def over_y(k, back):
        at = table.at[core, less(y, k) if back else y, x]
        return remote(at, at, sem2, 4 + k, ((y + k) % 4 * 4 + x, me))

    def relay_y(k, j, back):
        at = table.at[core, less(y, j) if back else y, less(x, k), pl.ds(0, 8)]
        return remote(at, at, sem2, 8 + (k - 1) * 3 + j - 1, ((y + j) % 4 * 4 + x, me))

    def relay_x(k, j, back):
        at = table.at[core, less(y, k), less(x, j) if back else x, pl.ds(8, 8)]
        return remote(at, at, sem2, 17 + (k - 1) * 3 + j - 1, (y * 4 + (x + j) % 4, me))

    def partner(dy, dx, back):
        at = table.at[1 - core if back else core, less(y, dy), less(x, dx)]
        return remote(at, at, sem3, dy * 4 + dx, (au, z * 2 + 1 - core))

    box[0, 0:16, :] = beam_ref[...].astype(F32)
    own_beam[...] = jnp.concatenate([box[0, pl.ds(0, 8, stride=2), :], box[0, pl.ds(1, 8, stride=2), :]], axis=0).astype(BF)
    own = pltpu.make_async_copy(own_beam, table.at[core, y, x, z], local_sem.at[0])
    own.start()
    pl.semaphore_wait(barrier, NV - 1 + NA - 1)
    loop(1, NZ, lambda k: along_z(k, False).start())
    step_setup(vis_ref, off_ref, scale_ref, vs, zu, mu, zv)
    step_sky(0, SPLIT, zu, mu, zv, wp, sky)
    own.wait()
    loop(1, NZ, lambda k: along_z(k, True).wait_recv())
    for k in (1, 2, 3):
        over_x(k, False).start()
        over_y(k, False).start()
    partner(0, 0, False).start()
    step_sky(SPLIT, 12, zu, mu, zv, wp, sky)
    for k in (1, 3, 2):
        over_x(k, True).wait_recv()
        for j in (1, 2, 3):
            relay_y(k, j, False).start()
        over_y(k, True).wait_recv()
        for j in (1, 2, 3):
            relay_x(k, j, False).start()
        partner(0, k, False).start()
        partner(k, 0, False).start()
    step_notes(au, corner_vec, lines, place)
    step_screen(corner_ref, depth_ref, sky, box)
    for dy in (1, 3, 2):
        for dx in (1, 3, 2):
            relay_y(dx, dy, True).wait_recv()
            relay_x(dy, dx, True).wait_recv()
            partner(dy, dx, False).start()
    for dy in range(4):
        for dx in range(4):
            partner(dy, dx, True).wait_recv()
    step_uv(station_ref, sky, table, lines, left_ref, right_ref, box, g_ref, rb)
    rows_send[...] = rb[...].reshape(32, 16, 128).astype(BF)

    def along_vert(send, recv, sems, k, back):
        peer = (me + NV - k) % NV if back else (me + k) % NV
        return remote(send.at[peer], recv.at[peer if back else me], sems, k, (au, peer))

    def across_au(send, recv, sems, k, back):
        peer = (au + NA - k) % NA if back else (au + k) % NA
        return remote(send.at[peer], recv.at[peer if back else au], sems, k, (peer, me))

    loop(1, NV, lambda k: along_vert(rows_send, rows_recv, sem4, k, False).start())
    rows_recv[me] = rows_send[me]
    step_slots(rb, place, slot_scr, slot_send)
    loop(1, NV, lambda k: along_vert(slot_send, slot_recv, sem5, k, False).start())
    slot_recv[me] = slot_send[me]
    loop(1, NV, lambda k: along_vert(rows_send, rows_recv, sem4, k, True).wait_recv())
    step_rows(me, rows_recv, stage1_ref, twist_ref, scr, lhs, oht, yv, turned)

    def half_across(low, k, back):
        peer = (au + NA - k) % NA if back else (au + k) % NA
        return remote(high_send.at[low, peer], high_recv.at[low, peer if back else au], sem6, low * NA + k, (peer, me))

    for low in range(2):
        step_split(low, stage2_ref, turned, buf, sbuf, high_send, spill_send)
        loop(1, NA, lambda k: half_across(low, k, False).start())
        high_recv[low, au] = high_send[low, au]
        if low == 0:
            loop(1, NA, lambda k: across_au(spill_send, spill_recv, sem7, k, False).start())
            spill_recv[au] = spill_send[au]
    loop(1, NA, lambda k: across_au(spill_send, spill_recv, sem7, k, True).wait_recv())
    for low in range(2):
        loop(1, NA, lambda k: half_across(low, k, True).wait_recv())
        step_high(me, low, high_recv, spill_recv, high_ref, xh, low_send)

        def send_low(k):
            @pl.when(((me + k) % NV) // 16 == low)
            def _():
                along_vert(low_send, low_recv, sem8, k, False).start()

        loop(1, NV, send_low)
    low_recv[me] = low_send[me]
    loop(1, NV, lambda k: along_vert(slot_send, slot_recv, sem5, k, True).wait_recv())
    step_tile(me, scr, slot_recv, slot_scr, spare, tile_ref, tail_send)
    tail = remote(tail_send, tail_recv, sem9, 0, ((au + 1) % NA, me))
    tail.start()
    tail.wait_recv()
    for k in range(4):
        tile_ref[pl.ds((k % 2) * 2 + k // 2, 32, stride=4), :] += tail_recv[k].astype(F32)
    put_tile = pltpu.make_async_copy(tile_ref, tile_out, local_sem.at[1])
    put_tile.start()
    loop(1, NV, lambda k: along_vert(low_send, low_recv, sem8, k, True).wait_recv())
    put_low = pltpu.make_async_copy(low_recv, low_out, local_sem.at[2])
    put_low.start()

    loop(1, NZ, lambda k: along_z(k, False).wait_send())
    for k in (1, 2, 3):
        over_x(k, False).wait_send()
        over_y(k, False).wait_send()
        for j in (1, 2, 3):
            relay_y(k, j, False).wait_send()
            relay_x(k, j, False).wait_send()
    for dy in range(4):
        for dx in range(4):
            partner(dy, dx, False).wait_send()
    loop(1, NV, lambda k: along_vert(rows_send, rows_recv, sem4, k, False).wait_send())
    loop(1, NV, lambda k: along_vert(slot_send, slot_recv, sem5, k, False).wait_send())
    for low in range(2):
        loop(1, NA, lambda k: half_across(low, k, False).wait_send())
    loop(1, NA, lambda k: across_au(spill_send, spill_recv, sem7, k, False).wait_send())
    loop(1, NV, lambda k: along_vert(low_send, low_recv, sem8, k, False).wait_send())
    tail.wait_send()
    put_tile.wait()
    put_low.wait()


def whole_call(corners, stations, depth, scale, vis, off, beam):
    left, right = dft_tables()
    stage1, twist, stage2 = row_tables()
    consts = [jnp.asarray(left, BF), jnp.asarray(right, BF), jnp.asarray(stage1, BF), jnp.asarray(twist, F32),
              jnp.asarray(stage2, BF), jnp.asarray(high_table(), BF)]
    V, D = pltpu.VMEM, pltpu.SemaphoreType.DMA
    scratch = [
        V((2, 4, 4, 16, 16, 128), BF), V((6, 16, 32, 128), F32), V((8, 16, 32, 128), F32), V((10, 16, 32, 128), F32), V((2, 128, NK), BF),
        V((NS, 64, 32), F32), V((WIDE, 64, 128), F32), V((NS * 64, 32), BF), V((512, 128), F32), V((32, 16, 128), BF), V((32, 16, 128), BF),
        V((512, 128), F32), V((NG * 64, 1536), BF), V((256, 1536), BF), V((NG * 64, 512), F32), V((4, 512, 128), F32), V((256, 128), F32),
        V((2, 16, 32, 256), BF), V((2, 16, 32, 256), BF), V((16, 16, 128), BF), V((16, 16, 128), BF), V((2, 512, 256), BF),
        V((32, 16, 512), BF), V((32, 16, 512), BF), V((1024, 128), F32), V((32, 32, 128), BF), V((32, 32, 128), BF),
        V((4, 256, 128), F32), V((4, 32, 128), BF), V((4, 32, 128), BF),
        V((768, 128), F32), V((8, 128), jnp.int32), V((64, 32), BF), V((16, 128), BF), V((NG * 64, 256), BF), V((2048, 128), F32),
        D((2, 16)), D((2, 32)), D((2, 16)), D((2, 32)), D((2, 32)), D((2, 32)), D((2, 16)), D((2, 32)), D((2, 1)), D((3,)),
    ]
    return pl.pallas_call(
        whole_kernel,
        out_shape=(jax.ShapeDtypeStruct((32, 16, 512), BF), jax.ShapeDtypeStruct((2048, 128), F32)),
        in_specs=[SM] * 4 + [VM] * 10, out_specs=(pl.BlockSpec(memory_space=pl.ANY),) * 2,
        scratch_shapes=scratch,
        compiler_params=pltpu.CompilerParams(collective_id=0, has_side_effects=True, vmem_limit_bytes=60 << 20),
        name="whole",
    )(corners, stations, depth, scale, corners, vis, off, beam, *consts)


def on_device(visibilities, baseline_offsets, channel_scale, screen_depth, stations, corners, beam_terms):
    low, tile = whole_call(
        corners.T, stations.T, screen_depth, channel_scale,
        visibilities.reshape(NS, 2, 16, 128).transpose(0, 2, 1, 3).reshape(768, 128),
        baseline_offsets.reshape(48, 128),
        beam_terms.reshape(2, 8, 128).transpose(1, 0, 2).reshape(16, 128),
    )
    dirty, tile = last_call(low, tile)
    gridded = tile.reshape(512, 2, 2, 128).transpose(0, 2, 1, 3).reshape(512, 2, 256)
    return gridded, dirty.reshape(16, 64, 2, 128).transpose(0, 2, 1, 3).reshape(16, 2, 8192)


def solution(mesh):
    from jax.sharding import PartitionSpec as P

    both = ("au", "vert")
    return jax.shard_map(
        on_device,
        mesh=mesh,
        in_specs=(P(both, None, None), P(both, None, None), P(), P(both), P(both, None), P(both, None), P(both, None, None)),
        out_specs=(P("au", None, "vert"), P(both, None, None)),
        check_vma=False,
    )
```
